32 devices in a mesh: dom: 8 (over y, x, core), head: 4 (over z).
Axes of the slice: x: 2, y: 2, z: 4, core: 2. Of those that a mesh axis runs over, the one named last changes fastest.
Arguments:
- features: bfloat16 [25, 128, 4096], P(None, None, ('dom', 'head')), may hold values from -14 to 14
- positions: float32 [3, 4096], P(None, 'dom'), may hold values from 0 to 3
- penalty: float32 [16], replicated, may hold values from 0.01 to 0.5
- qk_weight: bfloat16 [128, 2048], replicated, may hold values from -0.5 to 0.5
- value_weight: bfloat16 [5, 128, 128], replicated, may hold values from -0.5 to 0.5
- output_weight: bfloat16 [5, 128, 128], replicated, may hold values from -0.5 to 0.5
- frames: float32 [64, 25, 25], replicated, may hold values from -3 to 3, as said below
- frame_index: int32 [64], P('dom'), may hold values from 0 to 63
- neighbours: int32 [64, 8], P('dom'), may hold values from 0 to 63, as said below
- counts: int32 [64], P('dom'), may hold values from 1 to 8
- cotangent: bfloat16 [25, 128, 4096], P(None, None, ('dom', 'head')), may hold values from -6 to 6
Outputs:
- updated: bfloat16 [25, 128, 4096], P(None, None, ('dom', 'head'))
- forces: float32 [3, 4096], P(None, ('dom', 'head'))
The draws below stay inside these ranges and needn't reach their ends.
Inputs may be any that keep to these rules, and one draw needn't show every extreme that they name: `frames`: entries outside the diagonal blocks of components of one degree are zero. `neighbours`: row b holds 8 distinct blocks (b + o) mod 64 with |o| <= 4; the slots at and beyond counts[b] are padding.
All inputs are finite; a program needn't handle non-finite values.
Results may differ from the reference program's by a relative error of at most 0.0037.
The reference program's roundings to bfloat16 on the way count: a program that leaves them out, or rounds other values in their place, can miss the bound.
Values may be sent and summed in bfloat16 or wider, within the bound.
A program may use at most 64 MiB of HBM per device.

```python
import math
import jax
import jax.numpy as jnp
from jax import lax

COMP = 25
LDEG = 5
CH = 128
HEADS = 16
ALPHA = 64
BLOCK = 64
NBR = 8
REACH = 4
NFRAME = 64
ATOMS = 4096
BLOCKS = 64


def draw_features(key, part):
    folded = jax.random.fold_in(key, 101)
    first_key = jax.random.fold_in(folded, 0)
    return jnp.clip(jax.random.normal(first_key, (COMP, CH, ATOMS), jnp.float32), -6.0, 6.0).astype(jnp.bfloat16)


def draw_frames(key, part):
    folded = jax.random.fold_in(key, 202)
    index_comp = jnp.arange(COMP)
    degrees = jnp.sum((index_comp[:, None] >= (jnp.arange(1, LDEG) ** 2)[None, :]).astype(jnp.int32), axis=1)
    same_degree = (degrees[:, None] == degrees[None, :]).astype(jnp.float32)
    widths = jnp.sqrt(2.0 * degrees.astype(jnp.float32) + 1.0)[None, :, None]
    noise_draw = jnp.clip(jax.random.normal(folded, (NFRAME, COMP, COMP), jnp.float32), -4.0, 4.0)
    return (jnp.eye(COMP, dtype=jnp.float32)[None] + 0.5 * noise_draw / widths) * same_degree[None]


def draw_neighbours(key, part):
    folded = jax.random.fold_in(key, 303)
    spanned = 2 * REACH + 1
    raw_scores = jax.random.randint(folded, (BLOCKS, spanned), 0, 1 << 20) * spanned + jnp.arange(spanned)[None, :]
    ordering = jnp.argsort(raw_scores, axis=1)
    offsets = ordering[:, :NBR] - REACH
    return jnp.mod(jnp.arange(BLOCKS)[:, None] + offsets, BLOCKS).astype(jnp.int32)


def draw_counts(key, part):
    folded = jax.random.fold_in(key, 404)
    first_key, second_key, third_key = jax.random.split(folded, 3)
    values_drawn = jax.random.randint(first_key, (BLOCKS,), 1, NBR + 1)
    fullest = jax.random.randint(second_key, (), 0, BLOCKS)
    emptiest = jnp.mod(fullest + 1 + jax.random.randint(third_key, (), 0, BLOCKS - 1), BLOCKS)
    return values_drawn.at[fullest].set(NBR).at[emptiest].set(1).astype(jnp.int32)


def plant(result, own_key, smallest, largest):
    index_at = [jax.random.randint(jax.random.fold_in(own_key, axis), (), 0, length) for axis, length in enumerate(result.shape)]
    main_axis = result.shape.index(max(result.shape))
    beside = index_at[:main_axis] + [(index_at[main_axis] + 1) % result.shape[main_axis]] + index_at[main_axis + 1:]
    return result.at[tuple(index_at)].set(smallest).at[tuple(beside)].set(largest)


def shard_levels(key, extent, cuts, least, high):
    def one(axis_at, shards_of):
        heights = jax.random.uniform(jax.random.fold_in(jax.random.fold_in(key, 6), axis_at), (shards_of,), jnp.float32, least / len(cuts), high / len(cuts))
        return jnp.repeat(jnp.exp(heights), extent[axis_at] // shards_of).reshape((-1,) + (1,) * (len(extent) - axis_at - 1))

    loudness = one(*cuts[0])
    for cut in cuts[1:]:
        loudness = loudness * one(*cut)
    return loudness


def gaussian(rng, dims, deviation, most, cuts=(), kind=jnp.bfloat16):
    result = jax.random.normal(rng, dims, jnp.float32) * deviation
    if len(cuts) > 0:
        result = shard_levels(rng, dims, cuts, -0.22, 0.18) * result
    return jnp.clip(result, min=-most, max=most).astype(kind)


def setup_inputs(seed: int = 0) -> dict:
    streams_of = jax.random.split(jax.random.key(seed), 12)
    return {
        "features": draw_features(jax.random.fold_in(streams_of[11], 71), 0),
        "positions": jnp.clip(3.0 * jax.random.uniform(streams_of[1], (3, ATOMS), jnp.float32) ** shard_levels(streams_of[1], (3, ATOMS), ((1, 8),), -0.2, 0.2), 0.0, 3.0),
        "penalty": jnp.clip(jnp.exp(jax.random.uniform(streams_of[2], (HEADS,), jnp.float32, math.log(0.01), math.log(0.5))), 0.01, 0.5),
        "qk_weight": gaussian(streams_of[3], (CH, 2 * HEADS * ALPHA), CH ** -0.5, 0.5),
        "value_weight": gaussian(streams_of[4], (LDEG, CH, CH), CH ** -0.5, 0.5),
        "output_weight": gaussian(streams_of[5], (LDEG, CH, CH), CH ** -0.5, 0.5),
        "frames": draw_frames(jax.random.fold_in(streams_of[11], 71), 0),
        "frame_index": plant(jax.random.randint(streams_of[7], (BLOCKS,), 0, NFRAME), jax.random.fold_in(streams_of[7], 1), 0, NFRAME - 1).astype(jnp.int32),
        "neighbours": draw_neighbours(jax.random.fold_in(streams_of[11], 71), 0),
        "counts": draw_counts(jax.random.fold_in(streams_of[11], 71), 0),
        "cotangent": gaussian(streams_of[10], (COMP, CH, ATOMS), 1.0, 6.0, ((2, 32),)),
    }


NEG_FILL = -1e+30

def degree_table():
    components = jnp.arange(COMP)
    degrees = lax.optimization_barrier(jnp.sum((components[:, None] >= (jnp.arange(1, LDEG) ** 2)[None, :]).astype(jnp.int32), axis=1))
    orders = components - degrees * degrees - degrees
    return (jnp.abs(orders) <= 2).astype(jnp.float32)

def projectors(frames):
    kept_mask = degree_table()
    return jnp.einsum('fji,j,fjk->fik', frames, kept_mask, frames, precision=lax.Precision.HIGHEST)

def mix_degrees(operand, weights, reverse):
    pieces = []
    for degree in range(weights.shape[0]):
        sliced = operand[degree * degree:(degree + 1) * (degree + 1)].astype(jnp.float32)
        matrix = weights[degree].astype(jnp.float32)
        if reverse:
            pieces.append(jnp.einsum('koa,co->kca', sliced, matrix))
        else:
            pieces.append(jnp.einsum('kca,co->koa', sliced, matrix))
    return jnp.concatenate(pieces, 0)

def pick_group(nblocks, heads_here):
    chosen = 1
    for candidate in range(1, nblocks + 1):
        if nblocks % candidate == 0 and candidate * BLOCK * heads_here <= 512:
            chosen = candidate
    return chosen

def reference(features, positions, penalty, qk_weight, value_weight, output_weight, frames, frame_index, neighbours, counts, cotangent):
    atoms_all = features.shape[2]
    blocks_all = atoms_all // BLOCK
    head_width = CH // HEADS
    query_rows = HEADS * ALPHA
    projections = projectors(frames)
    queries_keys = jnp.dot(qk_weight.T, features[0], preferred_element_type=jnp.float32).astype(jnp.bfloat16)
    values = mix_degrees(features, value_weight, False).astype(jnp.bfloat16)
    grads = mix_degrees(cotangent, output_weight, True).astype(jnp.bfloat16)
    query_blocks = queries_keys[:query_rows].reshape(HEADS, ALPHA, blocks_all, BLOCK)
    key_blocks = queries_keys[query_rows:].reshape(HEADS, ALPHA, blocks_all, BLOCK)
    value_blocks = values.reshape(COMP, HEADS, head_width, blocks_all, BLOCK)
    grad_blocks = grads.reshape(COMP, HEADS, head_width, blocks_all, BLOCK)
    point_blocks = positions.reshape(3, blocks_all, BLOCK)
    usable = jnp.arange(NBR)[None, :] < counts[:, None]
    matrices = projections[frame_index]
    group_size = pick_group(blocks_all, 1)
    inverse_root = 1.0 / math.sqrt(ALPHA)

    def group_step(state_now, begin_at):
        attended_all, query_forces, ghost_forces = state_now
        slot_blocks = lax.dynamic_slice_in_dim(neighbours, begin_at, group_size, 0)
        query_group = lax.dynamic_slice_in_dim(query_blocks, begin_at, group_size, 2).astype(jnp.float32)
        key_group = jnp.take(key_blocks, slot_blocks, axis=2).astype(jnp.float32)
        value_group = jnp.take(value_blocks, slot_blocks, axis=3).astype(jnp.float32)
        grad_group = lax.dynamic_slice_in_dim(grad_blocks, begin_at, group_size, 3).astype(jnp.float32)
        query_points = lax.dynamic_slice_in_dim(point_blocks, begin_at, group_size, 1)
        key_points = jnp.take(point_blocks, slot_blocks, axis=1)
        live_slots = lax.dynamic_slice_in_dim(usable, begin_at, group_size, 0)
        group_mats = lax.dynamic_slice_in_dim(matrices, begin_at, group_size, 0)
        scores = jnp.einsum('hagi,hagsj->hgisj', query_group, key_group) * inverse_root
        separation = query_points[:, :, :, None, None] - key_points[:, :, None, :, :]
        distance = lax.optimization_barrier(jnp.sum(separation * separation, axis=0))
        logits = scores - penalty[:, None, None, None, None] * distance[None]
        slot_mask = live_slots[None, :, None, :, None]
        logits = jnp.where(slot_mask, logits, NEG_FILL)
        peaks = lax.optimization_barrier(jnp.max(logits, axis=(3, 4), keepdims=True))
        exponent = jnp.where(slot_mask, jnp.exp(logits - peaks), 0.0)
        attention = exponent / lax.optimization_barrier(jnp.sum(exponent, axis=(3, 4), keepdims=True))
        rounded = lax.optimization_barrier(attention.astype(jnp.bfloat16)).astype(jnp.float32)
        aggregate = jnp.einsum('hgisj,khdgsj->khdgi', rounded, value_group)
        attended = jnp.einsum('gkl,lhdgi->khdgi', group_mats, aggregate, precision=lax.Precision.HIGHEST).astype(jnp.bfloat16)
        rotated = jnp.einsum('glk,lhdgi->khdgi', group_mats, grad_group, precision=lax.Precision.HIGHEST)
        rotated = lax.optimization_barrier(rotated.astype(jnp.bfloat16)).astype(jnp.float32)
        weight_grads = jnp.einsum('khdgi,khdgsj->hgisj', rotated, value_group)
        logit_grads = attention * (weight_grads - lax.optimization_barrier(jnp.sum(attention * weight_grads, axis=(3, 4), keepdims=True)))
        total = lax.optimization_barrier(jnp.sum(2.0 * penalty[:, None, None, None, None] * logit_grads, axis=0))
        force_query = lax.optimization_barrier(jnp.sum(total[None] * separation, axis=(3, 4)))
        force_key = -lax.optimization_barrier(jnp.sum(total[None] * separation, axis=2))
        attended_all = lax.dynamic_update_slice_in_dim(attended_all, attended, begin_at, 3)
        query_forces = lax.dynamic_update_slice_in_dim(query_forces, force_query, begin_at, 1)
        ghost_forces = ghost_forces.at[:, slot_blocks.reshape(-1)].add(force_key.reshape(3, -1, BLOCK))
        return ((attended_all, query_forces, ghost_forces), None)
    initial = (jnp.zeros((COMP, HEADS, head_width, blocks_all, BLOCK), jnp.bfloat16), jnp.zeros((3, blocks_all, BLOCK), jnp.float32), jnp.zeros((3, blocks_all, BLOCK), jnp.float32))
    begins = jnp.arange(0, blocks_all, group_size).astype(jnp.int32)
    final_state, unused_out = lax.scan(group_step, initial, begins)
    attended_all, query_forces, ghost_forces = final_state
    attended_atoms = attended_all.reshape(COMP, CH, atoms_all)
    updated = (features.astype(jnp.float32) + mix_degrees(attended_atoms, output_weight, False)).astype(jnp.bfloat16)
    forces = (query_forces + ghost_forces).reshape(3, atoms_all)
    return (updated, forces)
```

```python
import functools
import math

import jax
import jax.numpy as jnp
import numpy as np
from jax import lax
from jax.experimental import pallas as pl
from jax.experimental.pallas import tpu as pltpu
from jax.sharding import PartitionSpec as P

BLOCK = 64
REACH = 4
FAR = 1e30
VMEM_LIMIT = 40 * 1024 * 1024


def degree_of(k):
    return math.isqrt(k)


def pair_table(comp):
    pairs = []
    for k in range(comp):
        l = degree_of(k)
        for m in range(l * l, (l + 1) * (l + 1)):
            pairs.append((k, m))
    return pairs


def vmem():
    return pl.BlockSpec(memory_space=pltpu.VMEM)


def dot(a, b, ca, cb):
    return lax.dot_general(
        a, b, (((ca,), (cb,)), ((), ())), preferred_element_type=jnp.float32
    )


def values_kernel(features, weight, out):
    comp = features.shape[0]
    ranks, rows, width, atoms = out.shape
    for k in range(comp):
        mixed = dot(weight[degree_of(k)], features[k], 0, 0)
        out[:, k] = mixed.reshape(ranks, width, atoms).astype(jnp.bfloat16)
    scalars = features[0].astype(jnp.float32).reshape(rows - comp, width, atoms)
    scalars = scalars.astype(jnp.bfloat16)
    for rank in range(ranks):
        out[rank, comp:] = scalars


def back_kernel(cotangent, weight, out):
    ranks, comp, width, atoms = out.shape
    for k in range(comp):
        mixed = dot(weight[degree_of(k)], cotangent[k], 1, 0)
        out[:, k] = mixed.reshape(ranks, width, atoms).astype(jnp.bfloat16)


def update_kernel(features, attended, weight, out):
    comp, channels, atoms = out.shape
    for k in range(comp):
        gathered = attended[:, k].astype(jnp.float32).reshape(channels, atoms)
        mixed = dot(weight[degree_of(k)], gathered.astype(jnp.bfloat16), 0, 0)
        out[k] = (features[k].astype(jnp.float32) + mixed).astype(jnp.bfloat16)


def attention_kernel(
    heads,
    alpha,
    comp,
    penalty,
    before,
    own,
    after,
    back,
    q_weight,
    k_weight,
    coef,
    mask,
    points,
    points_t,
    attended,
    forces,
    values_s,
    keys_s,
    queries_s,
    rotated_s,
    aggregate_s,
):
    step = pl.program_id(0)
    tiles, _, width, atoms = own.shape
    halo = before.shape[0]
    window = 2 * halo + 1
    head_width = width // heads
    channels = q_weight.shape[0]

    def prepare(ref, at, slot, with_query):
        tile = ref[at].astype(jnp.float32)
        for h in range(heads):
            part = tile[:comp, h * head_width : (h + 1) * head_width]
            values_s[slot, h] = part.reshape(comp * head_width, atoms).astype(jnp.bfloat16)
        scalars = tile[comp:].reshape(channels, atoms)
        keys = dot(k_weight[...], scalars.astype(jnp.bfloat16), 0, 0)
        keys_s[slot] = keys.reshape(heads, alpha, atoms).astype(jnp.bfloat16)
        if with_query:
            turned = scalars.T.astype(jnp.bfloat16)
            for h in range(heads):
                queries_s[at, h] = dot(turned, q_weight[:, h * alpha : (h + 1) * alpha], 1, 0).astype(
                    jnp.bfloat16
                )

    @pl.when(step == 0)
    def _():
        forces[...] = jnp.zeros_like(forces)

        def edge(i, carry):
            prepare(before, i, i, False)
            prepare(after, i, i + halo + tiles, False)
            return carry

        def inner(i, carry):
            prepare(own, i, i + halo, True)
            return carry

        lax.fori_loop(0, halo, edge, 0)
        lax.fori_loop(0, tiles, inner, 0)

    pairs = pair_table(comp)
    index_of = {pair: n for n, pair in enumerate(pairs)}

    def rotate(source, k, turned):
        l = degree_of(k)
        total = None
        for m in range(l * l, (l + 1) * (l + 1)):
            row = index_of[(m, k) if turned else (k, m)]
            term = coef[0, row : row + 1, :] * source(m)
            total = term if total is None else total + term
        return total

    for k in range(comp):
        rotated_s[k] = (
            rotate(lambda m: back[step, m].astype(jnp.float32), k, True)
            .astype(jnp.bfloat16)
            .astype(jnp.float32)
        )

    def windowed(get):
        return jnp.concatenate([get(step + w) for w in range(window)], axis=-1)

    rows = [windowed(lambda s, c=c: points[s, c : c + 1, :]) for c in range(3)]
    columns = [points_t[step, :, c : c + 1] for c in range(3)]
    distance = None
    for c in range(3):
        apart = columns[c] - rows[c]
        distance = apart * apart if distance is None else distance + apart * apart
    per_tile = atoms // BLOCK
    hidden = jnp.concatenate(
        [
            jnp.broadcast_to(mask[0, r : r + 1, :], (BLOCK, window * atoms))
            for r in range(per_tile)
        ],
        axis=0,
    )
    distance = jnp.maximum(distance, hidden)
    total = jnp.zeros((atoms, window * atoms), jnp.float32)
    scale = 1.0 / math.sqrt(alpha)
    for h in range(heads):
        strength = penalty[h]
        keys = windowed(lambda s: keys_s[s, h])
        values = windowed(lambda s: values_s[s, h])
        logits = dot(queries_s[step, h], keys, 1, 0) * scale - strength * distance
        peaks = jnp.max(logits, axis=1, keepdims=True)
        exponent = jnp.exp(logits - peaks)
        inverse = 1.0 / jnp.sum(exponent, axis=1, keepdims=True)
        attention = exponent * inverse
        aggregate = dot(values, attention.astype(jnp.bfloat16), 1, 1)
        aggregate_s[:, h * head_width : (h + 1) * head_width] = aggregate.reshape(
            comp, head_width, atoms
        )
        turned = rotated_s[:, h * head_width : (h + 1) * head_width].reshape(comp * head_width, atoms)
        weight_grads = dot(turned.T.astype(jnp.bfloat16), values, 1, 0)
        mean = jnp.sum(attention * weight_grads, axis=1, keepdims=True)
        total = total + (2.0 * strength) * (attention * (weight_grads - mean))
    for k in range(comp):
        attended[0, k] = rotate(lambda m: aggregate_s[m], k, False).astype(jnp.bfloat16)

    lane = lax.broadcasted_iota(jnp.int32, (atoms, atoms), 1)
    mine = jnp.zeros((atoms, atoms), jnp.float32)
    theirs = []
    for c in range(3):
        weighted = total * (columns[c] - rows[c])
        mine = jnp.where(lane == c, jnp.sum(weighted, axis=1, keepdims=True), mine)
        theirs.append(jnp.sum(weighted, axis=0, keepdims=True))
    mine = mine.T
    for c in range(3):
        forces[step + halo, c : c + 1, :] = forces[step + halo, c : c + 1, :] + mine[c : c + 1]
        for w in range(window):
            forces[step + w, c : c + 1, :] = (
                forces[step + w, c : c + 1, :] - theirs[c][:, w * atoms : (w + 1) * atoms]
            )


def on_device(
    features,
    positions,
    penalty,
    qk_weight,
    value_weight,
    output_weight,
    frames,
    frame_index,
    neighbours,
    counts,
    cotangent,
):
    comp, channels, atoms = features.shape
    ranks = lax.axis_size("head")
    doms = lax.axis_size("dom")
    heads_all = penalty.shape[0]
    heads = heads_all // ranks
    alpha = qk_weight.shape[1] // (2 * heads_all)
    width = channels // ranks
    tiles = positions.shape[1] // atoms
    per_tile = atoms // BLOCK
    halo = -(-REACH * BLOCK // atoms)
    window = 2 * halo + 1
    scalar_rows = channels // width
    head_width = width // heads
    slots = tiles + 2 * halo
    up = [(i, (i + 1) % doms) for i in range(doms)]
    down = [(j, i) for i, j in up]
    rank = lax.axis_index("head")
    params = pltpu.CompilerParams(vmem_limit_bytes=VMEM_LIMIT)
    mix_cost = pl.CostEstimate(
        flops=2 * comp * channels * channels * atoms,
        bytes_accessed=4 * comp * channels * atoms,
        transcendentals=0,
    )

    packed = pl.pallas_call(
        values_kernel,
        out_shape=jax.ShapeDtypeStruct((ranks, comp + scalar_rows, width, atoms), jnp.bfloat16),
        in_specs=[vmem()] * 2,
        out_specs=vmem(),
        compiler_params=params,
        cost_estimate=mix_cost,
        name="mix_values",
    )(features, value_weight)
    own = lax.all_to_all(packed, "head", split_axis=0, concat_axis=0, tiled=True)
    before = lax.ppermute(own[tiles - halo :], "dom", up)
    after = lax.ppermute(own[:halo], "dom", down)

    grads = pl.pallas_call(
        back_kernel,
        out_shape=jax.ShapeDtypeStruct((ranks, comp, width, atoms), jnp.bfloat16),
        in_specs=[vmem()] * 2,
        out_specs=vmem(),
        compiler_params=params,
        cost_estimate=mix_cost,
        name="mix_back",
    )(cotangent, output_weight)
    back = lax.all_to_all(grads, "head", split_axis=0, concat_axis=0, tiled=True)

    reach_atoms = halo * atoms
    last = lax.ppermute(positions[:, positions.shape[1] - reach_atoms :], "dom", up)
    first = lax.ppermute(positions[:, :reach_atoms], "dom", down)
    points = jnp.concatenate([last, positions, first], axis=1)
    points = points.reshape(3, slots, atoms).transpose(1, 0, 2)
    points_t = positions.reshape(3, tiles, atoms).transpose(1, 2, 0)

    chosen = jnp.take(frames, frame_index, axis=0)
    components = np.arange(comp)
    degrees = np.array([degree_of(k) for k in components])
    keep = np.abs(components - degrees * degrees - degrees) <= 2
    pairs = np.array(pair_table(comp))
    projections = jnp.einsum(
        "fji,j,fjk->fik",
        chosen,
        jnp.asarray(keep, jnp.float32),
        chosen,
        precision=lax.Precision.HIGHEST,
    )
    flat = projections.reshape(-1, comp * comp)
    picked = jnp.take(flat, jnp.asarray(pairs[:, 0] * comp + pairs[:, 1]), axis=1)
    coef = jnp.broadcast_to(
        picked.reshape(tiles, per_tile, -1).transpose(0, 2, 1)[..., None],
        (tiles, len(pairs), per_tile, BLOCK),
    ).reshape(tiles, len(pairs), atoms)

    blocks = neighbours.shape[0]
    block_ids = lax.axis_index("dom") * blocks + jnp.arange(blocks)
    offset = jnp.mod(neighbours - block_ids[:, None] + REACH, doms * blocks)
    usable = jnp.arange(neighbours.shape[1])[None, :] < counts[:, None]
    shift = jnp.arange(blocks) % per_tile + halo * per_tile - REACH
    place = offset + shift[:, None]
    hit = jnp.any(
        usable[:, :, None] & (place[:, :, None] == jnp.arange(window * per_tile)), axis=1
    )
    mask = jnp.broadcast_to(
        jnp.where(hit, 0.0, FAR).astype(jnp.float32)[..., None],
        (blocks, window * per_tile, BLOCK),
    ).reshape(tiles, per_tile, window * atoms)

    q_weight = lax.dynamic_slice_in_dim(qk_weight, rank * heads * alpha, heads * alpha, 1)
    k_weight = lax.dynamic_slice_in_dim(
        qk_weight, (heads_all + rank * heads) * alpha, heads * alpha, 1
    )
    penalty_here = lax.dynamic_slice_in_dim(penalty, rank * heads, heads)

    attended, forces = pl.pallas_call(
        functools.partial(attention_kernel, heads, alpha, comp),
        grid=(tiles,),
        out_shape=(
            jax.ShapeDtypeStruct((tiles, comp, width, atoms), jnp.bfloat16),
            jax.ShapeDtypeStruct((slots, 3, atoms), jnp.float32),
        ),
        in_specs=[pl.BlockSpec(memory_space=pltpu.SMEM)]
        + [vmem()] * 6
        + [
            pl.BlockSpec((1, len(pairs), atoms), lambda t: (t, 0, 0)),
            pl.BlockSpec((1, per_tile, window * atoms), lambda t: (t, 0, 0)),
            vmem(),
            vmem(),
        ],
        out_specs=(
            pl.BlockSpec((1, comp, width, atoms), lambda t: (t, 0, 0, 0)),
            vmem(),
        ),
        scratch_shapes=[
            pltpu.VMEM((slots, heads, comp * head_width, atoms), jnp.bfloat16),
            pltpu.VMEM((slots, heads, alpha, atoms), jnp.bfloat16),
            pltpu.VMEM((tiles, heads, atoms, alpha), jnp.bfloat16),
            pltpu.VMEM((comp, width, atoms), jnp.float32),
            pltpu.VMEM((comp, width, atoms), jnp.float32),
        ],
        compiler_params=params,
        name="attention",
    )(
        penalty_here,
        before,
        own,
        after,
        back,
        q_weight,
        k_weight,
        coef,
        mask,
        points,
        points_t,
    )

    arrived = lax.all_to_all(attended, "head", split_axis=0, concat_axis=0, tiled=True)
    low = lax.ppermute(forces[:halo], "dom", down)
    high = lax.ppermute(forces[slots - halo :], "dom", up)
    shared = forces[halo : halo + tiles]
    shared = shared + jnp.concatenate([high, jnp.zeros_like(shared[halo:])], axis=0)
    shared = shared + jnp.concatenate([jnp.zeros_like(shared[halo:]), low], axis=0)
    shares = lax.all_to_all(shared, "head", split_axis=0, concat_axis=0, tiled=True)
    force = jnp.sum(shares, axis=0)

    updated = pl.pallas_call(
        update_kernel,
        out_shape=jax.ShapeDtypeStruct(features.shape, jnp.bfloat16),
        in_specs=[vmem()] * 3,
        out_specs=vmem(),
        compiler_params=params,
        cost_estimate=mix_cost,
        name="update",
    )(features, arrived, output_weight)
    return (updated, force)


def solution(mesh):
    split = ("dom", "head")
    in_specs = (
        P(None, None, split),
        P(None, "dom"),
        P(),
        P(),
        P(),
        P(),
        P(),
        P("dom"),
        P("dom", None),
        P("dom"),
        P(None, None, split),
    )
    out_specs = (P(None, None, split), P(None, split))
    return jax.shard_map(
        on_device, mesh=mesh, in_specs=in_specs, out_specs=out_specs, check_vma=False
    )
```

```python
import functools
import math

import jax
import jax.numpy as jnp
import numpy as np
from jax import lax
from jax.experimental import pallas as pl
from jax.experimental.pallas import tpu as pltpu
from jax.sharding import PartitionSpec as P

BLOCK = 64
REACH = 4
FAR = 1e30
VMEM_LIMIT = 40 * 1024 * 1024


def degree_of(k):
    return math.isqrt(k)


def pair_table(comp):
    pairs = []
    for k in range(comp):
        l = degree_of(k)
        for m in range(l * l, (l + 1) * (l + 1)):
            pairs.append((k, m))
    return pairs


def vmem():
    return pl.BlockSpec(memory_space=pltpu.VMEM)


def dot(a, b, ca, cb):
    return lax.dot_general(
        a, b, (((ca,), (cb,)), ((), ())), preferred_element_type=jnp.float32
    )


def values_kernel(features, weight, out):
    comp = features.shape[0]
    ranks, rows, width, atoms = out.shape
    for k in range(comp):
        mixed = dot(weight[degree_of(k)], features[k], 0, 0)
        out[:, k] = mixed.reshape(ranks, width, atoms).astype(jnp.bfloat16)
    scalars = features[0].astype(jnp.float32).reshape(rows - comp, width, atoms)
    scalars = scalars.astype(jnp.bfloat16)
    for rank in range(ranks):
        out[rank, comp:] = scalars


def back_kernel(cotangent, weight, out):
    ranks, comp, width, atoms = out.shape
    for k in range(comp):
        mixed = dot(weight[degree_of(k)], cotangent[k], 1, 0)
        out[:, k] = mixed.reshape(ranks, width, atoms).astype(jnp.bfloat16)


def update_kernel(features, attended, weight, out):
    comp, channels, atoms = out.shape
    for k in range(comp):
        gathered = attended[:, k].astype(jnp.float32).reshape(channels, atoms)
        mixed = dot(weight[degree_of(k)], gathered.astype(jnp.bfloat16), 0, 0)
        out[k] = (features[k].astype(jnp.float32) + mixed).astype(jnp.bfloat16)


def rotated_rows(coef, comp, source, k, turned):
    index_of = {pair: n for n, pair in enumerate(pair_table(comp))}
    l = degree_of(k)
    total = None
    for m in range(l * l, (l + 1) * (l + 1)):
        row = index_of[(m, k) if turned else (k, m)]
        term = coef[0, row : row + 1, :] * source(m)
        total = term if total is None else total + term
    return total


def windowed(step, window, get):
    return jnp.concatenate([get(step + w) for w in range(window)], axis=-1)


def gather_kernel(
    heads,
    alpha,
    comp,
    penalty,
    before,
    own,
    after,
    q_weight,
    k_weight,
    coef,
    mask,
    points,
    points_t,
    attended,
    attention_out,
    values_s,
    keys_s,
    queries_s,
    aggregate_s,
):
    step = pl.program_id(0)
    tiles, _, width, atoms = own.shape
    halo = before.shape[0]
    window = 2 * halo + 1
    head_width = width // heads
    channels = q_weight.shape[0]

    def prepare(ref, at, slot, with_query):
        tile = ref[at].astype(jnp.float32)
        for h in range(heads):
            part = tile[:comp, h * head_width : (h + 1) * head_width]
            values_s[slot, h] = part.reshape(comp * head_width, atoms).astype(jnp.bfloat16)
        scalars = tile[comp:].reshape(channels, atoms)
        keys = dot(k_weight[...], scalars.astype(jnp.bfloat16), 0, 0)
        keys_s[slot] = keys.reshape(heads, alpha, atoms).astype(jnp.bfloat16)
        if with_query:
            turned = scalars.T.astype(jnp.bfloat16)
            for h in range(heads):
                queries_s[at, h] = dot(
                    turned, q_weight[:, h * alpha : (h + 1) * alpha], 1, 0
                ).astype(jnp.bfloat16)

    @pl.when(step == 0)
    def _():
        def edge(i, carry):
            prepare(before, i, i, False)
            prepare(after, i, i + halo + tiles, False)
            return carry

        def inner(i, carry):
            prepare(own, i, i + halo, True)
            return carry

        lax.fori_loop(0, halo, edge, 0)
        lax.fori_loop(0, tiles, inner, 0)

    distance = None
    for c in range(3):
        row = windowed(step, window, lambda s: points[s, c : c + 1, :])
        apart = points_t[step, :, c : c + 1] - row
        distance = apart * apart if distance is None else distance + apart * apart
    hidden = jnp.concatenate(
        [
            jnp.broadcast_to(mask[0, r : r + 1, :], (BLOCK, window * atoms))
            for r in range(atoms // BLOCK)
        ],
        axis=0,
    )
    distance = jnp.maximum(distance, hidden)
    scale = 1.0 / math.sqrt(alpha)
    for h in range(heads):
        keys = windowed(step, window, lambda s: keys_s[s, h])
        values = windowed(step, window, lambda s: values_s[s, h])
        logits = dot(queries_s[step, h], keys, 1, 0) * scale - penalty[h] * distance
        peaks = jnp.max(logits, axis=1, keepdims=True)
        exponent = jnp.exp(logits - peaks)
        inverse = 1.0 / jnp.sum(exponent, axis=1, keepdims=True)
        attention = exponent * inverse
        attention_out[0, h] = attention
        aggregate = dot(values, attention.astype(jnp.bfloat16), 1, 1)
        aggregate_s[:, h * head_width : (h + 1) * head_width] = aggregate.reshape(
            comp, head_width, atoms
        )
    for k in range(comp):
        attended[0, k] = rotated_rows(coef, comp, lambda m: aggregate_s[m], k, False).astype(
            jnp.bfloat16
        )


def force_kernel(
    heads,
    penalty,
    back,
    attention_in,
    values_s,
    coef,
    points,
    points_t,
    forces,
    rotated_s,
):
    step = pl.program_id(0)
    _, comp, width, atoms = back.shape
    head_width = width // heads
    window = attention_in.shape[3] // atoms
    halo = window // 2

    @pl.when(step == 0)
    def _():
        forces[...] = jnp.zeros_like(forces)

    for k in range(comp):
        rotated_s[k] = (
            rotated_rows(coef, comp, lambda m: back[0, m].astype(jnp.float32), k, True)
            .astype(jnp.bfloat16)
            .astype(jnp.float32)
        )
    total = jnp.zeros((atoms, window * atoms), jnp.float32)
    for h in range(heads):
        values = windowed(step, window, lambda s: values_s[s, h])
        attention = attention_in[0, h]
        turned = rotated_s[:, h * head_width : (h + 1) * head_width].reshape(
            comp * head_width, atoms
        )
        weight_grads = dot(turned.T.astype(jnp.bfloat16), values, 1, 0)
        mean = jnp.sum(attention * weight_grads, axis=1, keepdims=True)
        total = total + (2.0 * penalty[h]) * (attention * (weight_grads - mean))

    lane = lax.broadcasted_iota(jnp.int32, (atoms, atoms), 1)
    mine = jnp.zeros((atoms, atoms), jnp.float32)
    theirs = []
    for c in range(3):
        row = windowed(step, window, lambda s: points[s, c : c + 1, :])
        weighted = total * (points_t[step, :, c : c + 1] - row)
        mine = jnp.where(lane == c, jnp.sum(weighted, axis=1, keepdims=True), mine)
        theirs.append(jnp.sum(weighted, axis=0, keepdims=True))
    mine = mine.T
    for c in range(3):
        forces[step + halo, c : c + 1, :] = forces[step + halo, c : c + 1, :] + mine[c : c + 1]
        for w in range(window):
            forces[step + w, c : c + 1, :] = (
                forces[step + w, c : c + 1, :] - theirs[c][:, w * atoms : (w + 1) * atoms]
            )


def on_device(
    features,
    positions,
    penalty,
    qk_weight,
    value_weight,
    output_weight,
    frames,
    frame_index,
    neighbours,
    counts,
    cotangent,
):
    comp, channels, atoms = features.shape
    ranks = lax.axis_size("head")
    doms = lax.axis_size("dom")
    heads_all = penalty.shape[0]
    heads = heads_all // ranks
    alpha = qk_weight.shape[1] // (2 * heads_all)
    width = channels // ranks
    tiles = positions.shape[1] // atoms
    per_tile = atoms // BLOCK
    halo = -(-REACH * BLOCK // atoms)
    window = 2 * halo + 1
    scalar_rows = channels // width
    head_width = width // heads
    slots = tiles + 2 * halo
    up = [(i, (i + 1) % doms) for i in range(doms)]
    down = [(j, i) for i, j in up]
    rank = lax.axis_index("head")
    params = pltpu.CompilerParams(vmem_limit_bytes=VMEM_LIMIT)
    mix_cost = pl.CostEstimate(
        flops=2 * comp * channels * channels * atoms,
        bytes_accessed=4 * comp * channels * atoms,
        transcendentals=0,
    )

    packed = pl.pallas_call(
        values_kernel,
        out_shape=jax.ShapeDtypeStruct((ranks, comp + scalar_rows, width, atoms), jnp.bfloat16),
        in_specs=[vmem()] * 2,
        out_specs=vmem(),
        compiler_params=params,
        cost_estimate=mix_cost,
        name="mix_values",
    )(features, value_weight)
    own = lax.all_to_all(packed, "head", split_axis=0, concat_axis=0, tiled=True)
    before = lax.ppermute(own[tiles - halo :], "dom", up)
    after = lax.ppermute(own[:halo], "dom", down)

    grads = pl.pallas_call(
        back_kernel,
        out_shape=jax.ShapeDtypeStruct((ranks, comp, width, atoms), jnp.bfloat16),
        in_specs=[vmem()] * 2,
        out_specs=vmem(),
        compiler_params=params,
        cost_estimate=mix_cost,
        name="mix_back",
    )(cotangent, output_weight)
    back = lax.all_to_all(grads, "head", split_axis=0, concat_axis=0, tiled=True)

    reach_atoms = halo * atoms
    last = lax.ppermute(positions[:, positions.shape[1] - reach_atoms :], "dom", up)
    first = lax.ppermute(positions[:, :reach_atoms], "dom", down)
    points = jnp.concatenate([last, positions, first], axis=1)
    points = points.reshape(3, slots, atoms).transpose(1, 0, 2)
    points_t = positions.reshape(3, tiles, atoms).transpose(1, 2, 0)

    chosen = jnp.take(frames, frame_index, axis=0)
    components = np.arange(comp)
    degrees = np.array([degree_of(k) for k in components])
    keep = np.abs(components - degrees * degrees - degrees) <= 2
    pairs = np.array(pair_table(comp))
    projections = jnp.einsum(
        "fji,j,fjk->fik",
        chosen,
        jnp.asarray(keep, jnp.float32),
        chosen,
        precision=lax.Precision.HIGHEST,
    )
    flat = projections.reshape(-1, comp * comp)
    picked = jnp.take(flat, jnp.asarray(pairs[:, 0] * comp + pairs[:, 1]), axis=1)
    coef = jnp.broadcast_to(
        picked.reshape(tiles, per_tile, -1).transpose(0, 2, 1)[..., None],
        (tiles, len(pairs), per_tile, BLOCK),
    ).reshape(tiles, len(pairs), atoms)

    blocks = neighbours.shape[0]
    block_ids = lax.axis_index("dom") * blocks + jnp.arange(blocks)
    offset = jnp.mod(neighbours - block_ids[:, None] + REACH, doms * blocks)
    usable = jnp.arange(neighbours.shape[1])[None, :] < counts[:, None]
    shift = jnp.arange(blocks) % per_tile + halo * per_tile - REACH
    place = offset + shift[:, None]
    hit = jnp.any(
        usable[:, :, None] & (place[:, :, None] == jnp.arange(window * per_tile)), axis=1
    )
    mask = jnp.broadcast_to(
        jnp.where(hit, 0.0, FAR).astype(jnp.float32)[..., None],
        (blocks, window * per_tile, BLOCK),
    ).reshape(tiles, per_tile, window * atoms)

    q_weight = lax.dynamic_slice_in_dim(qk_weight, rank * heads * alpha, heads * alpha, 1)
    k_weight = lax.dynamic_slice_in_dim(
        qk_weight, (heads_all + rank * heads) * alpha, heads * alpha, 1
    )
    penalty_here = lax.dynamic_slice_in_dim(penalty, rank * heads, heads)

    smem = pl.BlockSpec(memory_space=pltpu.SMEM)
    coef_spec = pl.BlockSpec((1, len(pairs), atoms), lambda t: (t, 0, 0))
    tile_spec = pl.BlockSpec((1, comp, width, atoms), lambda t: (t, 0, 0, 0))
    weight_shape = (tiles, heads, atoms, window * atoms)
    weight_spec = pl.BlockSpec((1,) + weight_shape[1:], lambda t: (t, 0, 0, 0))
    half_cost = pl.CostEstimate(
        flops=4 * tiles * heads * comp * head_width * atoms * window * atoms,
        bytes_accessed=16 * 2**20,
        transcendentals=math.prod(weight_shape),
    )
    attended, attention, head_values = pl.pallas_call(
        functools.partial(gather_kernel, heads, alpha, comp),
        grid=(tiles,),
        out_shape=(
            jax.ShapeDtypeStruct((tiles, comp, width, atoms), jnp.bfloat16),
            jax.ShapeDtypeStruct(weight_shape, jnp.float32),
            jax.ShapeDtypeStruct((slots, heads, comp * head_width, atoms), jnp.bfloat16),
        ),
        in_specs=[smem]
        + [vmem()] * 5
        + [
            coef_spec,
            pl.BlockSpec((1, per_tile, window * atoms), lambda t: (t, 0, 0)),
            vmem(),
            vmem(),
        ],
        out_specs=(tile_spec, weight_spec, vmem()),
        scratch_shapes=[
            pltpu.VMEM((slots, heads, alpha, atoms), jnp.bfloat16),
            pltpu.VMEM((tiles, heads, atoms, alpha), jnp.bfloat16),
            pltpu.VMEM((comp, width, atoms), jnp.float32),
        ],
        compiler_params=params,
        cost_estimate=half_cost,
        name="aggregate",
    )(
        penalty_here,
        before,
        own,
        after,
        q_weight,
        k_weight,
        coef,
        mask,
        points,
        points_t,
    )
    forces = pl.pallas_call(
        functools.partial(force_kernel, heads),
        grid=(tiles,),
        out_shape=jax.ShapeDtypeStruct((slots, 3, atoms), jnp.float32),
        in_specs=[smem, tile_spec, weight_spec, vmem(), coef_spec, vmem(), vmem()],
        out_specs=vmem(),
        scratch_shapes=[pltpu.VMEM((comp, width, atoms), jnp.float32)],
        compiler_params=params,
        cost_estimate=half_cost,
        name="force_terms",
    )(penalty_here, back, attention, head_values, coef, points, points_t)

    arrived = lax.all_to_all(attended, "head", split_axis=0, concat_axis=0, tiled=True)
    low = lax.ppermute(forces[:halo], "dom", down)
    high = lax.ppermute(forces[slots - halo :], "dom", up)
    shared = forces[halo : halo + tiles]
    shared = shared + jnp.concatenate([high, jnp.zeros_like(shared[halo:])], axis=0)
    shared = shared + jnp.concatenate([jnp.zeros_like(shared[halo:]), low], axis=0)
    force = lax.dynamic_index_in_dim(shared, rank, 0, keepdims=False)
    for shift in range(1, ranks):
        share = lax.dynamic_index_in_dim(shared, (rank + shift) % ranks, 0, keepdims=False)
        force = force + lax.ppermute(
            share, "head", [(i, (i + shift) % ranks) for i in range(ranks)]
        )

    updated = pl.pallas_call(
        update_kernel,
        out_shape=jax.ShapeDtypeStruct(features.shape, jnp.bfloat16),
        in_specs=[vmem()] * 3,
        out_specs=vmem(),
        compiler_params=params,
        cost_estimate=mix_cost,
        name="update",
    )(features, arrived, output_weight)
    return (updated, force)


def solution(mesh):
    split = ("dom", "head")
    in_specs = (
        P(None, None, split),
        P(None, "dom"),
        P(),
        P(),
        P(),
        P(),
        P(),
        P("dom"),
        P("dom", None),
        P("dom"),
        P(None, None, split),
    )
    out_specs = (P(None, None, split), P(None, split))
    return jax.shard_map(
        on_device, mesh=mesh, in_specs=in_specs, out_specs=out_specs, check_vma=False
    )
```

```python
import functools
import math

import jax
import jax.numpy as jnp
from jax import lax
from jax.experimental import pallas as pl
from jax.experimental.pallas import tpu as pltpu
from jax.sharding import PartitionSpec as P

BLOCK = 64
REACH = 4
FAR = 1e30
VMEM_LIMIT = 40 * 1024 * 1024


def degree_of(k):
    return math.isqrt(k)


def pair_table(comp):
    pairs = []
    for k in range(comp):
        l = degree_of(k)
        for m in range(l * l, (l + 1) * (l + 1)):
            pairs.append((k, m))
    return pairs


def vmem():
    return pl.BlockSpec(memory_space=pltpu.VMEM)


def dot(a, b, ca, cb):
    return lax.dot_general(
        a, b, (((ca,), (cb,)), ((), ())), preferred_element_type=jnp.float32
    )


def rotated_rows(coef, tile, comp, source, k, turned):
    index_of = {pair: n for n, pair in enumerate(pair_table(comp))}
    l = degree_of(k)
    total = None
    for m in range(l * l, (l + 1) * (l + 1)):
        row = index_of[(m, k) if turned else (k, m)]
        term = coef[tile, row : row + 1, :] * source(m)
        total = term if total is None else total + term
    return total


def fused_kernel(
    heads,
    alpha,
    doms,
    ranks,
    halo,
    penalty,
    frame_index,
    neighbours,
    counts,
    features,
    cotangent,
    value_weight,
    output_weight,
    q_weight,
    k_weight,
    frames,
    own_points,
    updated,
    force,
    packed,
    ext,
    grads,
    back,
    finished,
    arrived,
    points,
    points_t,
    coef,
    mask,
    values_s,
    keys_s,
    queries_s,
    rotated_s,
    aggregate_s,
    attention_s,
    forces,
    from_low,
    from_high,
    shared,
    shares,
    value_sems,
    back_sems,
    finished_sems,
    share_sems,
    halo_sems,
    point_sems,
    rim_sems,
):
    comp, channels, atoms = features.shape
    tiles = own_points.shape[0]
    width = channels // ranks
    head_width = width // heads
    slots = tiles + 2 * halo
    window = 2 * halo + 1
    per_tile = atoms // BLOCK
    me = lax.axis_index("head")
    dom = lax.axis_index("dom")
    up = lax.rem(dom + 1, doms)
    down = lax.rem(dom + doms - 1, doms)

    def peer(shift):
        return lax.rem(me + shift, ranks)

    def source(shift):
        return lax.rem(me + ranks - shift, ranks)

    def remote(src, dst, sems, at, device):
        return pltpu.make_async_remote_copy(
            src_ref=src,
            dst_ref=dst,
            send_sem=sems.at[0, at],
            recv_sem=sems.at[1, at],
            device_id=device,
            device_id_type=pl.DeviceIdType.MESH,
        )

    barrier = pltpu.get_barrier_semaphore()
    for shift in range(1, ranks):
        pl.semaphore_signal(
            barrier, inc=1, device_id=(dom, peer(shift)), device_id_type=pl.DeviceIdType.MESH
        )
    for side in (up, down):
        pl.semaphore_signal(
            barrier, inc=1, device_id=(side, me), device_id_type=pl.DeviceIdType.MESH
        )

    for k in range(comp):
        mixed = dot(value_weight[degree_of(k)], features[k], 0, 0)
        packed[:, k] = mixed.reshape(ranks, width, atoms).astype(jnp.bfloat16)
    scalars = features[0].astype(jnp.float32).reshape(ranks, width, atoms).astype(jnp.bfloat16)
    for r in range(ranks):
        packed[r, comp:] = scalars

    pl.semaphore_wait(barrier, ranks + 1)

    value_copies = [
        remote(packed.at[peer(r)], ext.at[halo + me], value_sems, r, (dom, peer(r)))
        for r in range(1, ranks)
    ]
    for copy in value_copies:
        copy.start()
    point_copies = [
        remote(
            own_points.at[pl.ds(tiles - halo, halo)], points.at[pl.ds(0, halo)], point_sems, 0, (up, me)
        ),
        remote(
            own_points.at[pl.ds(0, halo)],
            points.at[pl.ds(halo + tiles, halo)],
            point_sems,
            1,
            (down, me),
        ),
    ]
    for copy in point_copies:
        copy.start()

    for k in range(comp):
        mixed = dot(output_weight[degree_of(k)], cotangent[k], 1, 0)
        grads[:, k] = mixed.reshape(ranks, width, atoms).astype(jnp.bfloat16)
    ext[halo + me] = packed[me]
    back[me] = grads[me]
    points[halo : halo + tiles] = own_points[...]

    components = lax.broadcasted_iota(jnp.int32, (comp, 1), 0)
    degrees = jnp.zeros_like(components)
    for l in range(1, degree_of(comp - 1) + 1):
        degrees = degrees + (components >= l * l).astype(jnp.int32)
    keep = (jnp.abs(components - degrees * degrees - degrees) <= 2).astype(jnp.float32)
    blocks = tiles * per_tile
    lane = lax.broadcasted_iota(jnp.int32, (1, atoms), 1)
    slot_of = lax.broadcasted_iota(jnp.int32, (1, window * atoms), 1) // BLOCK

    def tables(t, carry):
        points_t[t] = own_points[t].T
        matrices = []
        for r in range(per_tile):
            frame = frames[frame_index[t * per_tile + r]]
            matrices.append(
                lax.dot_general(
                    frame * keep,
                    frame,
                    (((0,), (0,)), ((), ())),
                    precision=lax.Precision.HIGHEST,
                    preferred_element_type=jnp.float32,
                )
            )
        at = 0
        for k in range(comp):
            l = degree_of(k)
            first, last = l * l, (l + 1) * (l + 1)
            rows = jnp.broadcast_to(matrices[0][first:last, k : k + 1], (last - first, atoms))
            for r in range(1, per_tile):
                here = jnp.broadcast_to(matrices[r][first:last, k : k + 1], (last - first, atoms))
                rows = jnp.where(lane < r * BLOCK, rows, here)
            coef[t, at : at + last - first, :] = rows
            at += last - first
        for r in range(per_tile):
            block = t * per_tile + r
            hidden = jnp.full((1, window * atoms), FAR, jnp.float32)
            shift = r + halo * per_tile - REACH
            for s in range(neighbours.shape[1]):
                offset = lax.rem(
                    neighbours[block, s] - (dom * blocks + block) + REACH + doms * blocks,
                    doms * blocks,
                )
                place = jnp.where(counts[block] > s, offset + shift, -1)
                hidden = jnp.where(slot_of == place, 0.0, hidden)
            mask[t, r : r + 1, :] = hidden
        return carry

    lax.fori_loop(0, tiles, tables, 0)

    for r in range(1, ranks):
        remote(packed.at[peer(r)], ext.at[halo + source(r)], value_sems, r, (dom, peer(r))).wait_recv()
    halo_copies = [
        remote(ext.at[pl.ds(tiles, halo)], ext.at[pl.ds(0, halo)], halo_sems, 0, (up, me)),
        remote(
            ext.at[pl.ds(halo, halo)], ext.at[pl.ds(halo + tiles, halo)], halo_sems, 1, (down, me)
        ),
    ]
    for copy in halo_copies:
        copy.start()
    back_copies = [
        remote(grads.at[peer(r)], back.at[me], back_sems, r, (dom, peer(r)))
        for r in range(1, ranks)
    ]
    for copy in back_copies:
        copy.start()

    def prepare(slot, with_query):
        tile = ext[slot].astype(jnp.float32)
        for h in range(heads):
            part = tile[:comp, h * head_width : (h + 1) * head_width]
            values_s[slot, h] = part.reshape(comp * head_width, atoms).astype(jnp.bfloat16)
        scalars = tile[comp:].reshape(channels, atoms)
        keys = dot(k_weight[...], scalars.astype(jnp.bfloat16), 0, 0)
        keys_s[slot] = keys.reshape(heads, alpha, atoms).astype(jnp.bfloat16)
        if with_query:
            turned = scalars.T.astype(jnp.bfloat16)
            for h in range(heads):
                queries_s[slot - halo, h] = dot(
                    turned, q_weight[:, h * alpha : (h + 1) * alpha], 1, 0
                ).astype(jnp.bfloat16)

    def inner(i, carry):
        prepare(i + halo, True)
        return carry

    lax.fori_loop(0, tiles, inner, 0)
    for copy in halo_copies + point_copies:
        copy.wait_recv()

    def edge(i, carry):
        prepare(i, False)
        prepare(i + halo + tiles, False)
        return carry

    lax.fori_loop(0, halo, edge, 0)

    def windowed(t, get):
        return jnp.concatenate([get(t + w) for w in range(window)], axis=-1)

    scale = 1.0 / math.sqrt(alpha)

    def send_finished(i):
        return remote(
            finished.at[peer(i)], arrived.at[me], finished_sems, i, (dom, peer(i))
        )

    def gather(i, carry):
        t = peer(i + 1)
        distance = None
        for c in range(3):
            row = windowed(t, lambda s: points[s, c : c + 1, :])
            apart = points_t[t, :, c : c + 1] - row
            distance = apart * apart if distance is None else distance + apart * apart
        hidden = jnp.concatenate(
            [
                jnp.broadcast_to(mask[t, r : r + 1, :], (BLOCK, window * atoms))
                for r in range(per_tile)
            ],
            axis=0,
        )
        distance = jnp.maximum(distance, hidden)

        @pl.when(i >= 1)
        def _():
            send_finished(i).start()

        for h in range(heads):
            keys = windowed(t, lambda s: keys_s[s, h])
            values = windowed(t, lambda s: values_s[s, h])
            strength = penalty[me * heads + h]
            logits = dot(queries_s[t, h], keys, 1, 0) * scale - strength * distance
            peaks = jnp.max(logits, axis=1, keepdims=True)
            exponent = jnp.exp(logits - peaks)
            inverse = 1.0 / jnp.sum(exponent, axis=1, keepdims=True)
            attention = exponent * inverse
            attention_s[t, h] = attention
            aggregate = dot(values, attention.astype(jnp.bfloat16), 1, 1)
            aggregate_s[:, h * head_width : (h + 1) * head_width] = aggregate.reshape(
                comp, head_width, atoms
            )
        for k in range(comp):
            finished[t, k] = rotated_rows(
                coef, t, comp, lambda m: aggregate_s[m], k, False
            ).astype(jnp.bfloat16)
        return carry

    lax.fori_loop(0, ranks, gather, 0)
    arrived[me] = finished[me]

    forces[...] = jnp.zeros_like(forces)
    for r in range(1, ranks):
        remote(grads.at[peer(r)], back.at[source(r)], back_sems, r, (dom, peer(r))).wait_recv()

    lane_square = lax.broadcasted_iota(jnp.int32, (atoms, atoms), 1)

    def terms(t, carry):
        for k in range(comp):
            rotated_s[k] = (
                rotated_rows(coef, t, comp, lambda m: back[t, m].astype(jnp.float32), k, True)
                .astype(jnp.bfloat16)
                .astype(jnp.float32)
            )
        total = jnp.zeros((atoms, window * atoms), jnp.float32)
        for h in range(heads):
            values = windowed(t, lambda s: values_s[s, h])
            attention = attention_s[t, h]
            turned = rotated_s[:, h * head_width : (h + 1) * head_width].reshape(
                comp * head_width, atoms
            )
            weight_grads = dot(turned.T.astype(jnp.bfloat16), values, 1, 0)
            mean = jnp.sum(attention * weight_grads, axis=1, keepdims=True)
            strength = penalty[me * heads + h]
            total = total + (2.0 * strength) * (attention * (weight_grads - mean))
        mine = jnp.zeros((atoms, atoms), jnp.float32)
        theirs = []
        for c in range(3):
            row = windowed(t, lambda s: points[s, c : c + 1, :])
            weighted = total * (points_t[t, :, c : c + 1] - row)
            mine = jnp.where(lane_square == c, jnp.sum(weighted, axis=1, keepdims=True), mine)
            theirs.append(jnp.sum(weighted, axis=0, keepdims=True))
        mine = mine.T
        for c in range(3):
            forces[t + halo, c : c + 1, :] = forces[t + halo, c : c + 1, :] + mine[c : c + 1]
            for w in range(window):
                forces[t + w, c : c + 1, :] = (
                    forces[t + w, c : c + 1, :] - theirs[c][:, w * atoms : (w + 1) * atoms]
                )
        return carry

    lax.fori_loop(0, tiles, terms, 0)

    rim_copies = [
        remote(forces.at[pl.ds(halo + tiles, halo)], from_low, rim_sems, 0, (up, me)),
        remote(forces.at[pl.ds(0, halo)], from_high, rim_sems, 1, (down, me)),
    ]
    for copy in rim_copies:
        copy.start()
    for copy in value_copies + halo_copies + point_copies + back_copies:
        copy.wait_send()
    for copy in rim_copies:
        copy.wait_recv()
    shared[...] = forces[halo : halo + tiles]
    shared[:halo] = shared[:halo] + from_low[...]
    shared[tiles - halo :] = shared[tiles - halo :] + from_high[...]
    shares[me] = shared[me]
    share_copies = [
        remote(shared.at[peer(r)], shares.at[me], share_sems, r, (dom, peer(r)))
        for r in range(1, ranks)
    ]
    for copy in share_copies:
        copy.start()

    for r in range(1, ranks):
        remote(
            finished.at[peer(r)], arrived.at[source(r)], finished_sems, r, (dom, peer(r))
        ).wait_recv()
    for k in range(comp):
        gathered = arrived[:, k].astype(jnp.float32).reshape(channels, atoms)
        mixed = dot(output_weight[degree_of(k)], gathered.astype(jnp.bfloat16), 0, 0)
        updated[k] = (features[k].astype(jnp.float32) + mixed).astype(jnp.bfloat16)

    for r in range(1, ranks):
        remote(
            shared.at[peer(r)], shares.at[source(r)], share_sems, r, (dom, peer(r))
        ).wait_recv()
    summed = shares[0]
    for r in range(1, ranks):
        summed = summed + shares[r]
    force[...] = summed[:3]
    for copy in rim_copies + share_copies:
        copy.wait_send()
    for r in range(1, ranks):
        send_finished(r).wait_send()


def on_device(
    features,
    positions,
    penalty,
    qk_weight,
    value_weight,
    output_weight,
    frames,
    frame_index,
    neighbours,
    counts,
    cotangent,
):
    comp, channels, atoms = features.shape
    ranks = lax.axis_size("head")
    doms = lax.axis_size("dom")
    heads_all = penalty.shape[0]
    heads = heads_all // ranks
    alpha = qk_weight.shape[1] // (2 * heads_all)
    width = channels // ranks
    tiles = positions.shape[1] // atoms
    per_tile = atoms // BLOCK
    halo = -(-REACH * BLOCK // atoms)
    window = 2 * halo + 1
    scalar_rows = channels // width
    head_width = width // heads
    slots = tiles + 2 * halo
    rank = lax.axis_index("head")
    table_rows = len(pair_table(comp))

    padded = jnp.pad(positions, ((0, 8 - positions.shape[0]), (0, 0)))
    own_points = padded.reshape(8, tiles, atoms).transpose(1, 0, 2)
    q_weight = lax.dynamic_slice_in_dim(qk_weight, rank * heads * alpha, heads * alpha, 1)
    k_weight = lax.dynamic_slice_in_dim(
        qk_weight, (heads_all + rank * heads) * alpha, heads * alpha, 1
    )
    bf16, f32 = jnp.bfloat16, jnp.float32
    smem = pl.BlockSpec(memory_space=pltpu.SMEM)
    dma = pltpu.SemaphoreType.DMA
    return pl.pallas_call(
        functools.partial(fused_kernel, heads, alpha, doms, ranks, halo),
        out_shape=(
            jax.ShapeDtypeStruct(features.shape, bf16),
            jax.ShapeDtypeStruct((positions.shape[0], atoms), f32),
        ),
        in_specs=[smem] * 4 + [vmem()] * 8,
        out_specs=(vmem(), vmem()),
        scratch_shapes=[
            pltpu.VMEM((ranks, comp + scalar_rows, width, atoms), bf16),
            pltpu.VMEM((slots, comp + scalar_rows, width, atoms), bf16),
            pltpu.VMEM((ranks, comp, width, atoms), bf16),
            pltpu.VMEM((tiles, comp, width, atoms), bf16),
            pltpu.VMEM((tiles, comp, width, atoms), bf16),
            pltpu.VMEM((ranks, comp, width, atoms), bf16),
            pltpu.VMEM((slots, 8, atoms), f32),
            pltpu.VMEM((tiles, atoms, 8), f32),
            pltpu.VMEM((tiles, table_rows, atoms), f32),
            pltpu.VMEM((tiles, per_tile, window * atoms), f32),
            pltpu.VMEM((slots, heads, comp * head_width, atoms), bf16),
            pltpu.VMEM((slots, heads, alpha, atoms), bf16),
            pltpu.VMEM((tiles, heads, atoms, alpha), bf16),
            pltpu.VMEM((comp, width, atoms), f32),
            pltpu.VMEM((comp, width, atoms), f32),
            pltpu.VMEM((tiles, heads, atoms, window * atoms), f32),
            pltpu.VMEM((slots, 8, atoms), f32),
            pltpu.VMEM((halo, 8, atoms), f32),
            pltpu.VMEM((halo, 8, atoms), f32),
            pltpu.VMEM((tiles, 8, atoms), f32),
            pltpu.VMEM((ranks, 8, atoms), f32),
            dma((2, ranks)),
            dma((2, ranks)),
            dma((2, ranks)),
            dma((2, ranks)),
            dma((2, 2)),
            dma((2, 2)),
            dma((2, 2)),
        ],
        compiler_params=pltpu.CompilerParams(
            vmem_limit_bytes=VMEM_LIMIT, collective_id=0, has_side_effects=True
        ),
        name="layer",
    )(
        penalty,
        frame_index,
        neighbours,
        counts,
        features,
        cotangent,
        value_weight,
        output_weight,
        q_weight,
        k_weight,
        frames,
        own_points,
    )


def solution(mesh):
    split = ("dom", "head")
    in_specs = (
        P(None, None, split),
        P(None, "dom"),
        P(),
        P(),
        P(),
        P(),
        P(),
        P("dom"),
        P("dom", None),
        P("dom"),
        P(None, None, split),
    )
    out_specs = (P(None, None, split), P(None, split))
    return jax.shard_map(
        on_device, mesh=mesh, in_specs=in_specs, out_specs=out_specs, check_vma=False
    )
```

```python
import functools
import math

import jax
import jax.numpy as jnp
from jax import lax
from jax.experimental import pallas as pl
from jax.experimental.pallas import tpu as pltpu
from jax.sharding import PartitionSpec as P

BLOCK = 64
REACH = 4
FAR = 1e30
VMEM_LIMIT = 63 * 1024 * 1024


def degree_of(k):
    return math.isqrt(k)


def pair_table(comp):
    pairs = []
    for k in range(comp):
        l = degree_of(k)
        for m in range(l * l, (l + 1) * (l + 1)):
            pairs.append((k, m))
    return pairs


def vmem():
    return pl.BlockSpec(memory_space=pltpu.VMEM)


def dot(a, b, ca, cb):
    return lax.dot_general(
        a, b, (((ca,), (cb,)), ((), ())), preferred_element_type=jnp.float32
    )


def rotated_rows(coef, tile, comp, source, k, turned):
    index_of = {pair: n for n, pair in enumerate(pair_table(comp))}
    l = degree_of(k)
    total = None
    for m in range(l * l, (l + 1) * (l + 1)):
        row = index_of[(m, k) if turned else (k, m)]
        term = coef[tile, row : row + 1, :] * source(m)
        total = term if total is None else total + term
    return total


def fused_kernel(
    heads,
    alpha,
    doms,
    ranks,
    halo,
    penalty,
    frame_index,
    neighbours,
    counts,
    features_in,
    cotangent_in,
    value_weight_in,
    output_weight_in,
    qk_weight_in,
    frames_in,
    positions_in,
    updated,
    force,
    packed,
    ext,
    grads,
    back,
    finished,
    arrived,
    points,
    points_t,
    coef,
    mask,
    values_s,
    keys_s,
    queries_s,
    rotated_s,
    aggregate_s,
    attention_s,
    forces,
    from_low,
    from_high,
    shared,
    shares,
    value_sems,
    back_sems,
    finished_sems,
    share_sems,
    halo_sems,
    point_sems,
    rim_sems,
    features,
    cotangent,
    value_weight,
    output_weight,
    qk_weight,
    frames,
    positions,
    q_weight,
    k_weight,
    own_points,
    load_sems,
):
    comp, channels, atoms = features.shape
    tiles = own_points.shape[0]
    width = channels // ranks
    head_width = width // heads
    slots = tiles + 2 * halo
    window = 2 * halo + 1
    per_tile = atoms // BLOCK
    me = lax.axis_index("head")
    dom = lax.axis_index("dom")
    up = lax.rem(dom + 1, doms)
    down = lax.rem(dom + doms - 1, doms)

    loads = [
        pltpu.make_async_copy(src, dst, load_sems.at[n])
        for n, (src, dst) in enumerate(
            [
                (features_in, features),
                (value_weight_in, value_weight),
                (positions_in, positions),
                (cotangent_in, cotangent),
                (output_weight_in, output_weight),
                (frames_in, frames),
                (qk_weight_in, qk_weight),
            ]
        )
    ]
    for load in loads:
        load.start()

    def peer(shift):
        return lax.rem(me + shift, ranks)

    def source(shift):
        return lax.rem(me + ranks - shift, ranks)

    def remote(src, dst, sems, at, device):
        return pltpu.make_async_remote_copy(
            src_ref=src,
            dst_ref=dst,
            send_sem=sems.at[0, at],
            recv_sem=sems.at[1, at],
            device_id=device,
            device_id_type=pl.DeviceIdType.MESH,
        )

    barrier = pltpu.get_barrier_semaphore()
    for shift in range(1, ranks):
        pl.semaphore_signal(
            barrier, inc=1, device_id=(dom, peer(shift)), device_id_type=pl.DeviceIdType.MESH
        )
    for side in (up, down):
        pl.semaphore_signal(
            barrier, inc=1, device_id=(side, me), device_id_type=pl.DeviceIdType.MESH
        )

    for load in loads[:3]:
        load.wait()
    own_points[...] = jnp.zeros_like(own_points)
    for t in range(tiles):
        own_points[t, : positions.shape[0]] = positions[:, t * atoms : (t + 1) * atoms]
    for k in range(comp):
        mixed = dot(value_weight[degree_of(k)], features[k], 0, 0)
        packed[:, k] = mixed.reshape(ranks, width, atoms).astype(jnp.bfloat16)
    scalars = features[0].astype(jnp.float32).reshape(ranks, width, atoms).astype(jnp.bfloat16)
    for r in range(ranks):
        packed[r, comp:] = scalars

    pl.semaphore_wait(barrier, ranks + 1)

    value_copies = [
        remote(packed.at[peer(r)], ext.at[halo + me], value_sems, r, (dom, peer(r)))
        for r in range(1, ranks)
    ]
    for copy in value_copies:
        copy.start()
    point_copies = [
        remote(
            own_points.at[pl.ds(tiles - halo, halo)], points.at[pl.ds(0, halo)], point_sems, 0, (up, me)
        ),
        remote(
            own_points.at[pl.ds(0, halo)],
            points.at[pl.ds(halo + tiles, halo)],
            point_sems,
            1,
            (down, me),
        ),
    ]
    for copy in point_copies:
        copy.start()

    for load in loads[3:]:
        load.wait()
    for k in range(comp):
        mixed = dot(output_weight[degree_of(k)], cotangent[k], 1, 0)
        grads[:, k] = mixed.reshape(ranks, width, atoms).astype(jnp.bfloat16)
    ext[halo + me] = packed[me]
    back[me] = grads[me]
    points[halo : halo + tiles] = own_points[...]

    head_columns = heads * alpha
    span = max(head_columns, 128)
    for part, target in enumerate((q_weight, k_weight)):
        at = part * ranks * head_columns + lax.div(me * head_columns, span) * span
        columns = qk_weight[:, pl.ds(pl.multiple_of(at, 128), span)]
        picked = columns[:, :head_columns]
        for n in range(1, span // head_columns):
            here = columns[:, n * head_columns : (n + 1) * head_columns]
            picked = jnp.where(lax.rem(me, span // head_columns) == n, here, picked)
        target[...] = picked

    blocks = tiles * per_tile
    lane = lax.broadcasted_iota(jnp.int32, (frames.shape[2], atoms), 1)
    frame_row = lax.broadcasted_iota(jnp.int32, (frames.shape[2], atoms), 0)
    slot_of = lax.broadcasted_iota(jnp.int32, (1, window * atoms), 1) // BLOCK

    def tables(t, carry):
        points_t[t] = own_points[t].T
        wanted = jnp.zeros_like(lane) + frame_index[t * per_tile]
        for r in range(1, per_tile):
            wanted = jnp.where(lane < r * BLOCK, wanted, frame_index[t * per_tile + r])
        onehot = (frame_row == wanted).astype(jnp.float32)
        at = 0
        for l in range(degree_of(comp - 1) + 1):
            first, last = l * l, (l + 1) * (l + 1)
            kept = [
                lax.dot_general(
                    frames[j],
                    onehot,
                    (((1,), (0,)), ((), ())),
                    precision=lax.Precision.HIGHEST,
                    preferred_element_type=jnp.float32,
                )
                for j in range(first, last)
                if abs(j - first - l) <= 2
            ]
            for k in range(first, last):
                rows = None
                for matrix in kept:
                    term = matrix[k : k + 1, :] * matrix[first:last, :]
                    rows = term if rows is None else rows + term
                coef[t, at : at + last - first, :] = rows
                at += last - first
        for r in range(per_tile):
            block = t * per_tile + r
            hidden = jnp.full((1, window * atoms), FAR, jnp.float32)
            shift = r + halo * per_tile - REACH
            for s in range(neighbours.shape[1]):
                offset = lax.rem(
                    neighbours[block, s] - (dom * blocks + block) + REACH + doms * blocks,
                    doms * blocks,
                )
                place = jnp.where(counts[block] > s, offset + shift, -1)
                hidden = jnp.where(slot_of == place, 0.0, hidden)
            mask[t, r : r + 1, :] = hidden
        return carry

    lax.fori_loop(0, tiles, tables, 0)

    back_copies = [
        remote(grads.at[peer(r)], back.at[me], back_sems, r, (dom, peer(r)))
        for r in range(1, ranks)
    ]
    for copy in back_copies:
        copy.start()

    for r in range(1, ranks):
        remote(packed.at[peer(r)], ext.at[halo + source(r)], value_sems, r, (dom, peer(r))).wait_recv()
    halo_copies = [
        remote(ext.at[pl.ds(tiles, halo)], ext.at[pl.ds(0, halo)], halo_sems, 0, (up, me)),
        remote(
            ext.at[pl.ds(halo, halo)], ext.at[pl.ds(halo + tiles, halo)], halo_sems, 1, (down, me)
        ),
    ]
    for copy in halo_copies:
        copy.start()
    def prepare(slot, with_query):
        tile = ext[slot].astype(jnp.float32)
        for h in range(heads):
            part = tile[:comp, h * head_width : (h + 1) * head_width]
            values_s[slot, h] = part.reshape(comp * head_width, atoms).astype(jnp.bfloat16)
        scalars = tile[comp:].reshape(channels, atoms)
        keys = dot(k_weight[...], scalars.astype(jnp.bfloat16), 0, 0)
        keys_s[slot] = keys.reshape(heads, alpha, atoms).astype(jnp.bfloat16)
        if with_query:
            turned = scalars.T.astype(jnp.bfloat16)
            for h in range(heads):
                queries_s[slot - halo, h] = dot(
                    turned, q_weight[:, h * alpha : (h + 1) * alpha], 1, 0
                ).astype(jnp.bfloat16)

    def inner(i, carry):
        prepare(i + halo, True)
        return carry

    lax.fori_loop(0, tiles, inner, 0)
    for copy in halo_copies + point_copies:
        copy.wait_recv()

    def edge(i, carry):
        prepare(i, False)
        prepare(i + halo + tiles, False)
        return carry

    lax.fori_loop(0, halo, edge, 0)

    def windowed(t, get):
        return jnp.concatenate([get(t + w) for w in range(window)], axis=-1)

    scale = 1.0 / math.sqrt(alpha)

    def send_finished(i):
        return remote(
            finished.at[peer(i)], arrived.at[me], finished_sems, i, (dom, peer(i))
        )

    def gather(i, carry):
        t = peer(i + 1)
        distance = None
        for c in range(3):
            row = windowed(t, lambda s: points[s, c : c + 1, :])
            apart = points_t[t, :, c : c + 1] - row
            distance = apart * apart if distance is None else distance + apart * apart
        hidden = jnp.concatenate(
            [
                jnp.broadcast_to(mask[t, r : r + 1, :], (BLOCK, window * atoms))
                for r in range(per_tile)
            ],
            axis=0,
        )
        distance = jnp.maximum(distance, hidden)

        @pl.when(i >= 1)
        def _():
            send_finished(i).start()

        for h in range(heads):
            keys = windowed(t, lambda s: keys_s[s, h])
            values = windowed(t, lambda s: values_s[s, h])
            strength = penalty[me * heads + h]
            logits = dot(queries_s[t, h], keys, 1, 0) * scale - strength * distance
            peaks = jnp.max(logits, axis=1, keepdims=True)
            exponent = jnp.exp(logits - peaks)
            inverse = 1.0 / jnp.sum(exponent, axis=1, keepdims=True)
            attention = exponent * inverse
            attention_s[t, h] = attention
            aggregate = dot(values, attention.astype(jnp.bfloat16), 1, 1)
            aggregate_s[:, h * head_width : (h + 1) * head_width] = aggregate.reshape(
                comp, head_width, atoms
            )
        for k in range(comp):
            finished[t, k] = rotated_rows(
                coef, t, comp, lambda m: aggregate_s[m], k, False
            ).astype(jnp.bfloat16)
        return carry

    lax.fori_loop(0, ranks, gather, 0)
    arrived[me] = finished[me]

    forces[...] = jnp.zeros_like(forces)
    for r in range(1, ranks):
        remote(grads.at[peer(r)], back.at[source(r)], back_sems, r, (dom, peer(r))).wait_recv()

    lane_square = lax.broadcasted_iota(jnp.int32, (atoms, atoms), 1)

    def terms(t, carry):
        for k in range(comp):
            rotated_s[k] = (
                rotated_rows(coef, t, comp, lambda m: back[t, m].astype(jnp.float32), k, True)
                .astype(jnp.bfloat16)
                .astype(jnp.float32)
            )
        total = jnp.zeros((atoms, window * atoms), jnp.float32)
        for h in range(heads):
            values = windowed(t, lambda s: values_s[s, h])
            attention = attention_s[t, h]
            turned = rotated_s[:, h * head_width : (h + 1) * head_width].reshape(
                comp * head_width, atoms
            )
            weight_grads = dot(turned.T.astype(jnp.bfloat16), values, 1, 0)
            mean = jnp.sum(attention * weight_grads, axis=1, keepdims=True)
            strength = penalty[me * heads + h]
            total = total + (2.0 * strength) * (attention * (weight_grads - mean))
        mine = jnp.zeros((atoms, atoms), jnp.float32)
        theirs = []
        for c in range(3):
            row = windowed(t, lambda s: points[s, c : c + 1, :])
            weighted = total * (points_t[t, :, c : c + 1] - row)
            mine = jnp.where(lane_square == c, jnp.sum(weighted, axis=1, keepdims=True), mine)
            theirs.append(jnp.sum(weighted, axis=0, keepdims=True))
        mine = mine.T
        for c in range(3):
            forces[t + halo, c : c + 1, :] = forces[t + halo, c : c + 1, :] + mine[c : c + 1]
            for w in range(window):
                forces[t + w, c : c + 1, :] = (
                    forces[t + w, c : c + 1, :] - theirs[c][:, w * atoms : (w + 1) * atoms]
                )
        return carry

    lax.fori_loop(0, tiles, terms, 0)

    rim_copies = [
        remote(forces.at[pl.ds(halo + tiles, halo)], from_low, rim_sems, 0, (up, me)),
        remote(forces.at[pl.ds(0, halo)], from_high, rim_sems, 1, (down, me)),
    ]
    for copy in rim_copies:
        copy.start()
    for copy in value_copies + halo_copies + point_copies + back_copies:
        copy.wait_send()
    for copy in rim_copies:
        copy.wait_recv()
    shared[...] = forces[halo : halo + tiles]
    shared[:halo] = shared[:halo] + from_low[...]
    shared[tiles - halo :] = shared[tiles - halo :] + from_high[...]
    shares[me] = shared[me]
    share_copies = [
        remote(shared.at[peer(r)], shares.at[me], share_sems, r, (dom, peer(r)))
        for r in range(1, ranks)
    ]
    for copy in share_copies:
        copy.start()

    for r in range(1, ranks):
        remote(
            finished.at[peer(r)], arrived.at[source(r)], finished_sems, r, (dom, peer(r))
        ).wait_recv()
    for k in range(comp):
        gathered = arrived[:, k].astype(jnp.float32).reshape(channels, atoms)
        mixed = dot(output_weight[degree_of(k)], gathered.astype(jnp.bfloat16), 0, 0)
        updated[k] = (features[k].astype(jnp.float32) + mixed).astype(jnp.bfloat16)

    for r in range(1, ranks):
        remote(
            shared.at[peer(r)], shares.at[source(r)], share_sems, r, (dom, peer(r))
        ).wait_recv()
    summed = shares[0]
    for r in range(1, ranks):
        summed = summed + shares[r]
    force[...] = summed[:3]
    for copy in rim_copies + share_copies:
        copy.wait_send()
    for r in range(1, ranks):
        send_finished(r).wait_send()


def on_device(
    features,
    positions,
    penalty,
    qk_weight,
    value_weight,
    output_weight,
    frames,
    frame_index,
    neighbours,
    counts,
    cotangent,
):
    comp, channels, atoms = features.shape
    ranks = lax.axis_size("head")
    doms = lax.axis_size("dom")
    heads_all = penalty.shape[0]
    heads = heads_all // ranks
    alpha = qk_weight.shape[1] // (2 * heads_all)
    width = channels // ranks
    tiles = positions.shape[1] // atoms
    per_tile = atoms // BLOCK
    halo = -(-REACH * BLOCK // atoms)
    window = 2 * halo + 1
    scalar_rows = channels // width
    head_width = width // heads
    slots = tiles + 2 * halo
    table_rows = len(pair_table(comp))

    framed = frames.transpose(1, 2, 0)
    bf16, f32 = jnp.bfloat16, jnp.float32
    smem = pl.BlockSpec(memory_space=pltpu.SMEM)
    dma = pltpu.SemaphoreType.DMA
    return pl.pallas_call(
        functools.partial(fused_kernel, heads, alpha, doms, ranks, halo),
        out_shape=(
            jax.ShapeDtypeStruct(features.shape, bf16),
            jax.ShapeDtypeStruct((positions.shape[0], atoms), f32),
        ),
        in_specs=[smem] * 4 + [pl.BlockSpec(memory_space=pltpu.MemorySpace.HBM)] * 7,
        out_specs=(vmem(), vmem()),
        scratch_shapes=[
            pltpu.VMEM((ranks, comp + scalar_rows, width, atoms), bf16),
            pltpu.VMEM((slots, comp + scalar_rows, width, atoms), bf16),
            pltpu.VMEM((ranks, comp, width, atoms), bf16),
            pltpu.VMEM((tiles, comp, width, atoms), bf16),
            pltpu.VMEM((tiles, comp, width, atoms), bf16),
            pltpu.VMEM((ranks, comp, width, atoms), bf16),
            pltpu.VMEM((slots, 8, atoms), f32),
            pltpu.VMEM((tiles, atoms, 8), f32),
            pltpu.VMEM((tiles, table_rows, atoms), f32),
            pltpu.VMEM((tiles, per_tile, window * atoms), f32),
            pltpu.VMEM((slots, heads, comp * head_width, atoms), bf16),
            pltpu.VMEM((slots, heads, alpha, atoms), bf16),
            pltpu.VMEM((tiles, heads, atoms, alpha), bf16),
            pltpu.VMEM((comp, width, atoms), f32),
            pltpu.VMEM((comp, width, atoms), f32),
            pltpu.VMEM((tiles, heads, atoms, window * atoms), f32),
            pltpu.VMEM((slots, 8, atoms), f32),
            pltpu.VMEM((halo, 8, atoms), f32),
            pltpu.VMEM((halo, 8, atoms), f32),
            pltpu.VMEM((tiles, 8, atoms), f32),
            pltpu.VMEM((ranks, 8, atoms), f32),
            dma((2, ranks)),
            dma((2, ranks)),
            dma((2, ranks)),
            dma((2, ranks)),
            dma((2, 2)),
            dma((2, 2)),
            dma((2, 2)),
            pltpu.VMEM(features.shape, bf16),
            pltpu.VMEM(cotangent.shape, bf16),
            pltpu.VMEM(value_weight.shape, bf16),
            pltpu.VMEM(output_weight.shape, bf16),
            pltpu.VMEM(qk_weight.shape, bf16),
            pltpu.VMEM(framed.shape, f32),
            pltpu.VMEM(positions.shape, f32),
            pltpu.VMEM((channels, heads * alpha), bf16),
            pltpu.VMEM((channels, heads * alpha), bf16),
            pltpu.VMEM((tiles, 8, atoms), f32),
            dma((7,)),
        ],
        compiler_params=pltpu.CompilerParams(
            vmem_limit_bytes=VMEM_LIMIT, collective_id=0, has_side_effects=True
        ),
        name="layer",
    )(
        penalty,
        frame_index,
        neighbours,
        counts,
        features,
        cotangent,
        value_weight,
        output_weight,
        qk_weight,
        framed,
        positions,
    )


def solution(mesh):
    split = ("dom", "head")
    in_specs = (
        P(None, None, split),
        P(None, "dom"),
        P(),
        P(),
        P(),
        P(),
        P(),
        P("dom"),
        P("dom", None),
        P("dom"),
        P(None, None, split),
    )
    out_specs = (P(None, None, split), P(None, split))
    return jax.shard_map(
        on_device, mesh=mesh, in_specs=in_specs, out_specs=out_specs, check_vma=False
    )
```

```python
import functools
import math

import jax
import jax.numpy as jnp
from jax import lax
from jax.experimental import pallas as pl
from jax.experimental.pallas import tpu as pltpu
from jax.sharding import PartitionSpec as P

BLOCK = 64
REACH = 4
FAR = 1e30
VMEM_LIMIT = 63 * 1024 * 1024


def degree_of(k):
    return math.isqrt(k)


def pair_table(comp):
    pairs = []
    for k in range(comp):
        l = degree_of(k)
        for m in range(l * l, (l + 1) * (l + 1)):
            pairs.append((k, m))
    return pairs


def vmem():
    return pl.BlockSpec(memory_space=pltpu.VMEM)


def dot(a, b, ca, cb):
    return lax.dot_general(
        a, b, (((ca,), (cb,)), ((), ())), preferred_element_type=jnp.float32
    )


def rotated_rows(coef, tile, comp, source, k, turned):
    index_of = {pair: n for n, pair in enumerate(pair_table(comp))}
    l = degree_of(k)
    total = None
    for m in range(l * l, (l + 1) * (l + 1)):
        row = index_of[(m, k) if turned else (k, m)]
        term = coef[tile, row : row + 1, :] * source(m)
        total = term if total is None else total + term
    return total


def fused_kernel(
    heads,
    alpha,
    doms,
    ranks,
    halo,
    penalty,
    frame_index,
    neighbours,
    counts,
    features_in,
    cotangent_in,
    value_weight_in,
    output_weight_in,
    qk_weight_in,
    frames_in,
    positions_in,
    updated,
    force,
    packed,
    ext,
    grads,
    back,
    finished,
    arrived,
    points,
    points_t,
    coef,
    mask,
    values_s,
    keys_s,
    queries_s,
    rotated_s,
    aggregate_s,
    attention_s,
    forces,
    from_low,
    from_high,
    shared,
    shares,
    value_sems,
    back_sems,
    finished_sems,
    share_sems,
    halo_sems,
    point_sems,
    rim_sems,
    features,
    cotangent,
    value_weight,
    output_weight,
    qk_weight,
    frames,
    positions,
    q_weight,
    k_weight,
    own_points,
    load_sems,
):
    comp, channels, atoms = features.shape
    tiles = own_points.shape[0]
    width = channels // ranks
    head_width = width // heads
    slots = tiles + 2 * halo
    window = 2 * halo + 1
    per_tile = atoms // BLOCK
    me = lax.axis_index("head")
    dom = lax.axis_index("dom")
    up = lax.rem(dom + 1, doms)
    down = lax.rem(dom + doms - 1, doms)

    loads = [
        pltpu.make_async_copy(src, dst, load_sems.at[n])
        for n, (src, dst) in enumerate(
            [
                (features_in, features),
                (value_weight_in, value_weight),
                (positions_in, positions),
                (cotangent_in, cotangent),
                (output_weight_in, output_weight),
                (frames_in, frames),
                (qk_weight_in, qk_weight),
            ]
        )
    ]
    for load in loads:
        load.start()

    def peer(shift):
        return lax.rem(me + shift, ranks)

    def source(shift):
        return lax.rem(me + ranks - shift, ranks)

    def remote(src, dst, sems, at, device):
        return pltpu.make_async_remote_copy(
            src_ref=src,
            dst_ref=dst,
            send_sem=sems.at[0, at],
            recv_sem=sems.at[1, at],
            device_id=device,
            device_id_type=pl.DeviceIdType.MESH,
        )

    barrier = pltpu.get_barrier_semaphore()
    for shift in range(1, ranks):
        pl.semaphore_signal(
            barrier, inc=1, device_id=(dom, peer(shift)), device_id_type=pl.DeviceIdType.MESH
        )
    for side in (up, down):
        pl.semaphore_signal(
            barrier, inc=1, device_id=(side, me), device_id_type=pl.DeviceIdType.MESH
        )

    for load in loads[:3]:
        load.wait()
    own_points[...] = jnp.zeros_like(own_points)
    for t in range(tiles):
        own_points[t, : positions.shape[0]] = positions[:, t * atoms : (t + 1) * atoms]
    for k in range(comp):
        mixed = dot(value_weight[degree_of(k)], features[k], 0, 0)
        packed[:, k] = mixed.reshape(ranks, width, atoms).astype(jnp.bfloat16)
    scalars = features[0].astype(jnp.float32).reshape(ranks, width, atoms).astype(jnp.bfloat16)
    for r in range(ranks):
        packed[r, comp:] = scalars

    pl.semaphore_wait(barrier, ranks + 1)

    value_copies = [
        remote(packed.at[peer(r)], ext.at[halo + me], value_sems, r, (dom, peer(r)))
        for r in range(1, ranks)
    ]
    for copy in value_copies:
        copy.start()
    point_copies = [
        remote(
            own_points.at[pl.ds(tiles - halo, halo)], points.at[pl.ds(0, halo)], point_sems, 0, (up, me)
        ),
        remote(
            own_points.at[pl.ds(0, halo)],
            points.at[pl.ds(halo + tiles, halo)],
            point_sems,
            1,
            (down, me),
        ),
    ]
    for copy in point_copies:
        copy.start()

    for load in loads[3:]:
        load.wait()
    for k in range(comp):
        mixed = dot(output_weight[degree_of(k)], cotangent[k], 1, 0)
        grads[:, k] = mixed.reshape(ranks, width, atoms).astype(jnp.bfloat16)
    ext[halo + me] = packed[me]
    back[me] = grads[me]
    points[halo : halo + tiles] = own_points[...]

    head_columns = heads * alpha
    span = max(head_columns, 128)
    for part, target in enumerate((q_weight, k_weight)):
        at = part * ranks * head_columns + lax.div(me * head_columns, span) * span
        columns = qk_weight[:, pl.ds(pl.multiple_of(at, 128), span)]
        picked = columns[:, :head_columns]
        for n in range(1, span // head_columns):
            here = columns[:, n * head_columns : (n + 1) * head_columns]
            picked = jnp.where(lax.rem(me, span // head_columns) == n, here, picked)
        target[...] = picked

    blocks = tiles * per_tile
    lane = lax.broadcasted_iota(jnp.int32, (frames.shape[2], atoms), 1)
    frame_row = lax.broadcasted_iota(jnp.int32, (frames.shape[2], atoms), 0)
    slot_of = lax.broadcasted_iota(jnp.int32, (1, window * atoms), 1) // BLOCK

    def tables(t, carry):
        points_t[t] = own_points[t].T
        wanted = jnp.zeros_like(lane) + frame_index[t * per_tile]
        for r in range(1, per_tile):
            wanted = jnp.where(lane < r * BLOCK, wanted, frame_index[t * per_tile + r])
        onehot = (frame_row == wanted).astype(jnp.float32)
        at = 0
        for l in range(degree_of(comp - 1) + 1):
            first, last = l * l, (l + 1) * (l + 1)
            kept = [
                lax.dot_general(
                    frames[j],
                    onehot,
                    (((1,), (0,)), ((), ())),
                    precision=lax.Precision.HIGHEST,
                    preferred_element_type=jnp.float32,
                )
                for j in range(first, last)
                if abs(j - first - l) <= 2
            ]
            for k in range(first, last):
                rows = None
                for matrix in kept:
                    term = matrix[k : k + 1, :] * matrix[first:last, :]
                    rows = term if rows is None else rows + term
                coef[t, at : at + last - first, :] = rows
                at += last - first
        for r in range(per_tile):
            block = t * per_tile + r
            hidden = jnp.full((1, window * atoms), FAR, jnp.float32)
            shift = r + halo * per_tile - REACH
            for s in range(neighbours.shape[1]):
                offset = lax.rem(
                    neighbours[block, s] - (dom * blocks + block) + REACH + doms * blocks,
                    doms * blocks,
                )
                place = jnp.where(counts[block] > s, offset + shift, -1)
                hidden = jnp.where(slot_of == place, 0.0, hidden)
            mask[t, r : r + 1, :] = hidden
        return carry

    lax.fori_loop(0, tiles, tables, 0)

    for r in range(1, ranks):
        remote(packed.at[peer(r)], ext.at[halo + source(r)], value_sems, r, (dom, peer(r))).wait_recv()
    halo_copies = [
        remote(ext.at[pl.ds(tiles, halo)], ext.at[pl.ds(0, halo)], halo_sems, 0, (up, me)),
        remote(
            ext.at[pl.ds(halo, halo)], ext.at[pl.ds(halo + tiles, halo)], halo_sems, 1, (down, me)
        ),
    ]
    for copy in halo_copies:
        copy.start()
    back_copies = [
        remote(grads.at[peer(r)], back.at[me], back_sems, r, (dom, peer(r)))
        for r in range(1, ranks)
    ]
    for copy in back_copies:
        copy.start()

    def prepare(slot, with_query):
        tile = ext[slot].astype(jnp.float32)
        for h in range(heads):
            part = tile[:comp, h * head_width : (h + 1) * head_width]
            values_s[slot, h] = part.reshape(comp * head_width, atoms).astype(jnp.bfloat16)
        scalars = tile[comp:].reshape(channels, atoms)
        keys = dot(k_weight[...], scalars.astype(jnp.bfloat16), 0, 0)
        keys_s[slot] = keys.reshape(heads, alpha, atoms).astype(jnp.bfloat16)
        if with_query:
            turned = scalars.T.astype(jnp.bfloat16)
            for h in range(heads):
                queries_s[slot - halo, h] = dot(
                    turned, q_weight[:, h * alpha : (h + 1) * alpha], 1, 0
                ).astype(jnp.bfloat16)

    def inner(i, carry):
        prepare(i + halo, True)
        return carry

    lax.fori_loop(0, tiles, inner, 0)
    for copy in halo_copies + point_copies:
        copy.wait_recv()

    def edge(i, carry):
        prepare(i, False)
        prepare(i + halo + tiles, False)
        return carry

    lax.fori_loop(0, halo, edge, 0)

    def windowed(t, get):
        return jnp.concatenate([get(t + w) for w in range(window)], axis=-1)

    scale = 1.0 / math.sqrt(alpha)

    def send_finished(i):
        return remote(
            finished.at[peer(i)], arrived.at[me], finished_sems, i, (dom, peer(i))
        )

    def gather(i, carry):
        t = peer(i + 1)
        distance = None
        for c in range(3):
            row = windowed(t, lambda s: points[s, c : c + 1, :])
            apart = points_t[t, :, c : c + 1] - row
            distance = apart * apart if distance is None else distance + apart * apart
        hidden = jnp.concatenate(
            [
                jnp.broadcast_to(mask[t, r : r + 1, :], (BLOCK, window * atoms))
                for r in range(per_tile)
            ],
            axis=0,
        )
        distance = jnp.maximum(distance, hidden)

        @pl.when(i >= 1)
        def _():
            send_finished(i).start()

        for h in range(heads):
            keys = windowed(t, lambda s: keys_s[s, h])
            values = windowed(t, lambda s: values_s[s, h])
            strength = penalty[me * heads + h]
            logits = dot(queries_s[t, h], keys, 1, 0) * scale - strength * distance
            peaks = jnp.max(logits, axis=1, keepdims=True)
            exponent = jnp.exp(logits - peaks)
            inverse = 1.0 / jnp.sum(exponent, axis=1, keepdims=True)
            attention = exponent * inverse
            attention_s[t, h] = attention
            aggregate = dot(values, attention.astype(jnp.bfloat16), 1, 1)
            aggregate_s[:, h * head_width : (h + 1) * head_width] = aggregate.reshape(
                comp, head_width, atoms
            )
        for k in range(comp):
            finished[t, k] = rotated_rows(
                coef, t, comp, lambda m: aggregate_s[m], k, False
            ).astype(jnp.bfloat16)
        return carry

    lax.fori_loop(0, ranks, gather, 0)
    arrived[me] = finished[me]

    forces[...] = jnp.zeros_like(forces)
    for r in range(1, ranks):
        remote(grads.at[peer(r)], back.at[source(r)], back_sems, r, (dom, peer(r))).wait_recv()

    lane_square = lax.broadcasted_iota(jnp.int32, (atoms, atoms), 1)

    def terms(t, carry):
        for k in range(comp):
            rotated_s[k] = (
                rotated_rows(coef, t, comp, lambda m: back[t, m].astype(jnp.float32), k, True)
                .astype(jnp.bfloat16)
                .astype(jnp.float32)
            )
        total = jnp.zeros((atoms, window * atoms), jnp.float32)
        for h in range(heads):
            values = windowed(t, lambda s: values_s[s, h])
            attention = attention_s[t, h]
            turned = rotated_s[:, h * head_width : (h + 1) * head_width].reshape(
                comp * head_width, atoms
            )
            weight_grads = dot(turned.T.astype(jnp.bfloat16), values, 1, 0)
            mean = jnp.sum(attention * weight_grads, axis=1, keepdims=True)
            strength = penalty[me * heads + h]
            total = total + (2.0 * strength) * (attention * (weight_grads - mean))
        mine = jnp.zeros((atoms, atoms), jnp.float32)
        theirs = []
        for c in range(3):
            row = windowed(t, lambda s: points[s, c : c + 1, :])
            weighted = total * (points_t[t, :, c : c + 1] - row)
            mine = jnp.where(lane_square == c, jnp.sum(weighted, axis=1, keepdims=True), mine)
            theirs.append(jnp.sum(weighted, axis=0, keepdims=True))
        mine = mine.T
        for c in range(3):
            forces[t + halo, c : c + 1, :] = forces[t + halo, c : c + 1, :] + mine[c : c + 1]
            for w in range(window):
                forces[t + w, c : c + 1, :] = (
                    forces[t + w, c : c + 1, :] - theirs[c][:, w * atoms : (w + 1) * atoms]
                )
        return carry

    lax.fori_loop(0, tiles, terms, 0)

    rim_copies = [
        remote(forces.at[pl.ds(halo + tiles, halo)], from_low, rim_sems, 0, (up, me)),
        remote(forces.at[pl.ds(0, halo)], from_high, rim_sems, 1, (down, me)),
    ]
    for copy in rim_copies:
        copy.start()
    for copy in value_copies + halo_copies + point_copies + back_copies:
        copy.wait_send()
    for copy in rim_copies:
        copy.wait_recv()
    shared[...] = forces[halo : halo + tiles]
    shared[:halo] = shared[:halo] + from_low[...]
    shared[tiles - halo :] = shared[tiles - halo :] + from_high[...]
    shares[me] = shared[me]
    share_copies = [
        remote(shared.at[peer(r)], shares.at[me], share_sems, r, (dom, peer(r)))
        for r in range(1, ranks)
    ]
    for copy in share_copies:
        copy.start()

    for r in range(1, ranks):
        remote(
            finished.at[peer(r)], arrived.at[source(r)], finished_sems, r, (dom, peer(r))
        ).wait_recv()
    for k in range(comp):
        gathered = arrived[:, k].astype(jnp.float32).reshape(channels, atoms)
        mixed = dot(output_weight[degree_of(k)], gathered.astype(jnp.bfloat16), 0, 0)
        updated[k] = (features[k].astype(jnp.float32) + mixed).astype(jnp.bfloat16)

    for r in range(1, ranks):
        remote(
            shared.at[peer(r)], shares.at[source(r)], share_sems, r, (dom, peer(r))
        ).wait_recv()
    summed = shares[0]
    for r in range(1, ranks):
        summed = summed + shares[r]
    force[...] = summed[:3]
    for copy in rim_copies + share_copies:
        copy.wait_send()
    for r in range(1, ranks):
        send_finished(r).wait_send()


def on_device(
    features,
    positions,
    penalty,
    qk_weight,
    value_weight,
    output_weight,
    frames,
    frame_index,
    neighbours,
    counts,
    cotangent,
):
    comp, channels, atoms = features.shape
    ranks = lax.axis_size("head")
    doms = lax.axis_size("dom")
    heads_all = penalty.shape[0]
    heads = heads_all // ranks
    alpha = qk_weight.shape[1] // (2 * heads_all)
    width = channels // ranks
    tiles = positions.shape[1] // atoms
    per_tile = atoms // BLOCK
    halo = -(-REACH * BLOCK // atoms)
    window = 2 * halo + 1
    scalar_rows = channels // width
    head_width = width // heads
    slots = tiles + 2 * halo
    table_rows = len(pair_table(comp))

    framed = frames.transpose(1, 2, 0)
    bf16, f32 = jnp.bfloat16, jnp.float32
    smem = pl.BlockSpec(memory_space=pltpu.SMEM)
    dma = pltpu.SemaphoreType.DMA
    return pl.pallas_call(
        functools.partial(fused_kernel, heads, alpha, doms, ranks, halo),
        out_shape=(
            jax.ShapeDtypeStruct(features.shape, bf16),
            jax.ShapeDtypeStruct((positions.shape[0], atoms), f32),
        ),
        in_specs=[smem] * 4 + [pl.BlockSpec(memory_space=pltpu.MemorySpace.HBM)] * 7,
        out_specs=(vmem(), vmem()),
        scratch_shapes=[
            pltpu.VMEM((ranks, comp + scalar_rows, width, atoms), bf16),
            pltpu.VMEM((slots, comp + scalar_rows, width, atoms), bf16),
            pltpu.VMEM((ranks, comp, width, atoms), bf16),
            pltpu.VMEM((tiles, comp, width, atoms), bf16),
            pltpu.VMEM((tiles, comp, width, atoms), bf16),
            pltpu.VMEM((ranks, comp, width, atoms), bf16),
            pltpu.VMEM((slots, 8, atoms), f32),
            pltpu.VMEM((tiles, atoms, 8), f32),
            pltpu.VMEM((tiles, table_rows, atoms), f32),
            pltpu.VMEM((tiles, per_tile, window * atoms), f32),
            pltpu.VMEM((slots, heads, comp * head_width, atoms), bf16),
            pltpu.VMEM((slots, heads, alpha, atoms), bf16),
            pltpu.VMEM((tiles, heads, atoms, alpha), bf16),
            pltpu.VMEM((comp, width, atoms), f32),
            pltpu.VMEM((comp, width, atoms), f32),
            pltpu.VMEM((tiles, heads, atoms, window * atoms), f32),
            pltpu.VMEM((slots, 8, atoms), f32),
            pltpu.VMEM((halo, 8, atoms), f32),
            pltpu.VMEM((halo, 8, atoms), f32),
            pltpu.VMEM((tiles, 8, atoms), f32),
            pltpu.VMEM((ranks, 8, atoms), f32),
            dma((2, ranks)),
            dma((2, ranks)),
            dma((2, ranks)),
            dma((2, ranks)),
            dma((2, 2)),
            dma((2, 2)),
            dma((2, 2)),
            pltpu.VMEM(features.shape, bf16),
            pltpu.VMEM(cotangent.shape, bf16),
            pltpu.VMEM(value_weight.shape, bf16),
            pltpu.VMEM(output_weight.shape, bf16),
            pltpu.VMEM(qk_weight.shape, bf16),
            pltpu.VMEM(framed.shape, f32),
            pltpu.VMEM(positions.shape, f32),
            pltpu.VMEM((channels, heads * alpha), bf16),
            pltpu.VMEM((channels, heads * alpha), bf16),
            pltpu.VMEM((tiles, 8, atoms), f32),
            dma((7,)),
        ],
        compiler_params=pltpu.CompilerParams(
            vmem_limit_bytes=VMEM_LIMIT, collective_id=0, has_side_effects=True
        ),
        name="layer",
    )(
        penalty,
        frame_index,
        neighbours,
        counts,
        features,
        cotangent,
        value_weight,
        output_weight,
        qk_weight,
        framed,
        positions,
    )


def solution(mesh):
    split = ("dom", "head")
    in_specs = (
        P(None, None, split),
        P(None, "dom"),
        P(),
        P(),
        P(),
        P(),
        P(),
        P("dom"),
        P("dom", None),
        P("dom"),
        P(None, None, split),
    )
    out_specs = (P(None, None, split), P(None, split))
    return jax.shard_map(
        on_device, mesh=mesh, in_specs=in_specs, out_specs=out_specs, check_vma=False
    )
```
